256 devices in a mesh: blk: 64 (over z, x_hi, y), par: 4 (over x_lo, core).
Axes of the slice: x: 4 (x_hi: 2, x_lo: 2; x = x_hi * 2 + x_lo), y: 4, z: 8, core: 2. Of those that a mesh axis runs over, the one named last changes fastest.
Arguments:
- log_derivs: float32 [16384, 4096], P('blk', 'par'), may hold values from -0.09375 to 0.09375
- energies: float32 [16384], P('blk'), may hold values from -6 to 6
Outputs:
- panel_tiles: float32 [16384, 256], P('blk')
- energies_next: float32 [16384], P('blk')
- diagonal_next: float32 [16384, 256], P(('blk', 'par'))
- neighbour_next: float32 [16384, 256], P(('blk', 'par'))
The draws below stay inside these ranges and needn't reach their ends.
All inputs are finite; a program needn't handle non-finite values.
Results may differ from the reference program's by a relative error of at most 0.00011.
Values sent between devices are 32-bit elements; how exact they have to be, the bound alone decides.
No kernel may reach another device: no remote copies, remote signals or barrier semaphores. Data moves between devices by JAX's collectives and lax.ppermute only.
A program may use at most 64 MiB of HBM per device.

```python
import jax
import jax.numpy as jnp
from jax import lax

P_SIZE = 4096
B = 256
NS = 16384


def levels(own_key, extent, pieces, low, high):
    loudness = 1.0
    for position, blocks in pieces:
        heights = jax.random.uniform(jax.random.fold_in(jax.random.fold_in(own_key, 6), position), (blocks,), jnp.float32, low / len(pieces), high / len(pieces))
        loudness = loudness * jnp.repeat(jnp.exp(heights), extent[position] // blocks).reshape((-1,) + (1,) * (len(extent) - 1 - position))
    return loudness


def bell_draw(own_key, dims, width, reach, split=(), held_as=jnp.bfloat16):
    gain = levels(own_key, dims, split, -0.22, 0.18) if split else 1.0
    drawn = jax.random.normal(own_key, dims, jnp.float32) * width * gain
    return jnp.minimum(jnp.maximum(drawn, -reach), reach).astype(held_as)


def setup_inputs(seed: int = 0) -> dict:
    seeds = jax.random.split(jax.random.key(seed), 3)
    return {
        "log_derivs": bell_draw(seeds[0], (NS, P_SIZE), P_SIZE ** -0.5, 0.09375, ((0, 64), (1, 4)), jnp.float32),
        "energies": bell_draw(seeds[1], (NS,), 1.0, 6.0, ((0, 64),), jnp.float32),
    }


ridge_shift = 0.05

def kernel_tile(left_rows, right_rows):
    return jnp.dot(left_rows.astype(jnp.float32), right_rows.T.astype(jnp.float32), precision=lax.Precision.HIGHEST, preferred_element_type=jnp.float32)

def reference(log_derivs, energies):
    block_count = NS // B
    sample_blocks = log_derivs.reshape(block_count, B, P_SIZE)
    lead_rows = sample_blocks[0]
    unit_rows = jnp.eye(B, dtype=jnp.float32)
    pivot_factor = jnp.linalg.cholesky(kernel_tile(lead_rows, lead_rows) + ridge_shift * unit_rows)

    def panel_of(block_rows):
        cross_tile = kernel_tile(block_rows, lead_rows)
        return lax.linalg.triangular_solve(pivot_factor, cross_tile, left_side=False, lower=True, transpose_a=True)
    previous_blocks = jnp.roll(sample_blocks, 1, axis=0)

    def per_block(block_pair):
        block_rows, prev_block = block_pair
        panel_here = panel_of(block_rows)
        panel_prev = panel_of(prev_block)
        diag_tile = kernel_tile(block_rows, block_rows) + ridge_shift * unit_rows - kernel_tile(panel_here, panel_here)
        cycle_tile = kernel_tile(block_rows, prev_block) - kernel_tile(panel_here, panel_prev)
        return (panel_here, diag_tile, cycle_tile)
    panels, diagonals, neighbours = lax.map(per_block, (sample_blocks, previous_blocks))
    panel_tiles = panels.reshape(NS, B)
    lead_solve = lax.linalg.triangular_solve(pivot_factor, energies[:B][:, None], left_side=True, lower=True)[:, 0]
    remainder = energies - jnp.dot(panel_tiles.astype(jnp.float32), lead_solve.astype(jnp.float32), precision=lax.Precision.HIGHEST, preferred_element_type=jnp.float32)
    energies_next = jnp.concatenate([lead_solve, remainder[B:]])
    return (panel_tiles, energies_next, diagonals.reshape(NS, B), neighbours.reshape(NS, B))
```

```python
import functools

import jax
import jax.numpy as jnp
from jax import lax
from jax.experimental import pallas as pl
from jax.experimental.pallas import tpu as pltpu
from jax.sharding import Mesh
from jax.sharding import PartitionSpec as P

BLK = ("z", "xh", "y")
PLANE = ("xh", "y")
PAR = ("xl", "core")
ALL = BLK + PAR
HIGHEST = lax.Precision.HIGHEST

ridge_shift = 0.05
CHUNK = 64


def dot(a, b, ca, cb):
    return lax.dot_general(
        a, b, (((ca,), (cb,)), ((), ())), precision=HIGHEST, preferred_element_type=jnp.float32
    )


def outer_tile(left_rows, right_rows):
    return dot(left_rows, right_rows, 1, 1)


def unit(rows, columns):
    return lax.broadcasted_iota(jnp.int32, (rows, columns), 0) == lax.broadcasted_iota(
        jnp.int32, (rows, columns), 1
    )


def triangle_inverse(tile):
    n = tile.shape[0]
    held = jnp.concatenate([tile, unit(n, n).astype(jnp.float32)], axis=1)
    rows = lax.broadcasted_iota(jnp.int32, held.shape, 0)
    for j in range(0, n, 2):
        low = (j // 8) * 8
        part, at = held[low:, :], rows[low:]
        first = jnp.broadcast_to(part[:, j : j + 1], part.shape)
        second = jnp.broadcast_to(part[:, j + 1 : j + 2], part.shape)
        row_a, row_b = held[j : j + 1, :], held[j + 1 : j + 2, :]
        k = j - low
        a, b, c = first[k : k + 1], first[k + 1 : k + 2], second[k + 1 : k + 2]
        over_a = 1.0 / a
        over_det = 1.0 / (a * c - b * b)
        t = b * over_a
        row_b = row_b - t * row_a
        update = first * over_a * row_a + (second - first * t) * (a * over_det) * row_b
        update = jnp.where(at > j + 1, update, 0.0)
        update = jnp.where(at == j + 1, jnp.broadcast_to(t * row_a, part.shape), update)
        part = part - update
        held = jnp.concatenate([held[:low], part], axis=0) if low else part
    pivots = jnp.sum(jnp.where(unit(n, 2 * n), held, 0.0), axis=1, keepdims=True)
    return held[:, n:] * (1.0 / jnp.sqrt(pivots))


def factor_inverse(tile_ref, inverse_ref):
    n = tile_ref.shape[0]
    inverse_ref[...] = jnp.zeros((n, n), jnp.float32)
    for r0 in range(0, n, CHUNK):
        r1 = r0 + CHUNK
        small = triangle_inverse(tile_ref[r0:r1, r0:r1])
        if r0:
            inverse_ref[r0:r1, :r0] = dot(small, inverse_ref[r0:r1, :r0], 1, 0)
        inverse_ref[r0:r1, r0:r1] = small
        if r1 < n:
            across = dot(small, tile_ref[r0:r1, r1:], 1, 0)
            tile_ref[r1:, r1:] = tile_ref[r1:, r1:] - dot(across, across, 0, 0)
            inverse_ref[r1:, :r1] = inverse_ref[r1:, :r1] - dot(
                across, inverse_ref[r0:r1, :r1], 0, 0
            )


def finish_kernel(
    at_ref, sums_ref, self_ref, cycle_ref, energy_ref, lead_ref,
    panel_ref, energies_ref, diagonal_ref, neighbour_ref, tile_ref, inverse_ref, prev_ref,
):
    n = tile_ref.shape[0]
    share = self_ref.shape[0]
    tile_ref[...] = sums_ref[2] + ridge_shift * unit(n, n).astype(jnp.float32)
    factor_inverse(tile_ref, inverse_ref)
    inverse = inverse_ref[...]
    panel = outer_tile(sums_ref[0], inverse)
    panel_ref[...] = panel
    prev_ref[...] = outer_tile(sums_ref[1], inverse)
    start = pl.multiple_of(at_ref[0] * share, share)
    own = panel_ref[pl.ds(start, share), :]
    shifted = (
        lax.broadcasted_iota(jnp.int32, (share, n), 0) + start
        == lax.broadcasted_iota(jnp.int32, (share, n), 1)
    ).astype(jnp.float32)
    diagonal_ref[...] = self_ref[...] + ridge_shift * shifted - outer_tile(own, panel)
    neighbour_ref[...] = cycle_ref[...] - outer_tile(own, prev_ref[...])
    lead = outer_tile(jnp.broadcast_to(lead_ref[...], (8, n)), inverse)
    remainder = energy_ref[...] - outer_tile(lead, panel)[:1]
    energies_ref[...] = jnp.where(at_ref[1] == 0, lead[:1], remainder)


def finish(at, sums, self_rows, cycle_rows, energies, lead_energy):
    n = sums.shape[-1]
    share = self_rows.shape[0]
    f32 = lambda *shape: jax.ShapeDtypeStruct(shape, jnp.float32)
    vmem = pl.BlockSpec(memory_space=pltpu.VMEM)
    return pl.pallas_call(
        finish_kernel,
        out_shape=(f32(n, n), f32(1, n), f32(share, n), f32(share, n)),
        in_specs=[pl.BlockSpec(memory_space=pltpu.SMEM)] + [vmem] * 5,
        out_specs=(vmem,) * 4,
        scratch_shapes=[pltpu.VMEM((n, n), jnp.float32)] * 3,
        name="finish",
    )(at, sums, self_rows, cycle_rows, energies, lead_energy)


def swapped(value, axis):
    return lax.ppermute(value, axis, [(0, 1), (1, 0)])


def passed_along(block, axis, distance):
    count = lax.axis_size(axis)
    return lax.ppermute(block, axis, [((i - distance) % count, i) for i in range(count)])


def sum_scattered(partials):
    k, n = partials.shape[0], partials.shape[-1]
    quarters = partials.reshape(k, 2, 2, n // 4, n)
    core, xl = lax.axis_index("core"), lax.axis_index("xl")
    pick = lambda a, i, d: lax.dynamic_index_in_dim(a, i, d, keepdims=False)
    halves = pick(quarters, core, 2) + swapped(pick(quarters, 1 - core, 2), "core")
    return pick(halves, xl, 1) + swapped(pick(halves, 1 - xl, 1), "xl")


def sum_everywhere(partials):
    k, n = partials.shape[0], partials.shape[-1]
    core = lax.axis_index("core")
    chip = partials + swapped(partials, "core")
    halves = chip.reshape(k, 2, n // 2, n)
    own = lax.dynamic_index_in_dim(halves, core, 1, keepdims=False)
    own = own + swapped(own, "xl")
    other = swapped(own, "core")
    upper = jnp.where(core == 0, own, other)
    lower = jnp.where(core == 0, other, own)
    return jnp.stack([upper, lower], axis=1).reshape(k, n, n)


def from_first(pieces, axis):
    count = lax.axis_size(axis)
    got = [lax.ppermute(pieces(k), axis, [(0, k)]) for k in range(1, count)]
    return jnp.where(lax.axis_index(axis) == 0, pieces(0), functools.reduce(jnp.add, got))


def broadcast_lead(rows):
    n = rows.shape[0]
    parts = lax.axis_size(PLANE)
    part = n // parts
    got = [
        lax.ppermute(rows[k * part : (k + 1) * part], BLK, [(0, k)]) for k in range(1, parts)
    ]
    piece = jnp.where(lax.axis_index(PLANE) == 0, rows[:part], functools.reduce(jnp.add, got))
    piece = from_first(lambda k: piece, "z")
    copies = jnp.broadcast_to(piece, (parts, *piece.shape))
    return lax.all_to_all(copies, PLANE, split_axis=0, concat_axis=0, tiled=True).reshape(rows.shape)


def on_device(log_derivs, energies):
    n = log_derivs.shape[0]
    width = log_derivs.shape[1]
    column = jnp.pad(energies[:, None], ((0, 0), (0, 127)))
    lead = broadcast_lead(jnp.concatenate([log_derivs, column], axis=1))
    lead_rows, lead_energy = lead[:, :width], lead[:, width].reshape(1, n)
    prev_rows = passed_along(log_derivs, BLK, 1)
    early = sum_scattered(
        jnp.stack([outer_tile(log_derivs, log_derivs), outer_tile(log_derivs, prev_rows)])
    )
    sums = sum_everywhere(
        jnp.stack(
            [
                outer_tile(log_derivs, lead_rows),
                outer_tile(prev_rows, lead_rows),
                outer_tile(lead_rows, lead_rows),
            ]
        )
    )
    at = jnp.stack([lax.axis_index(PAR), lax.axis_index(BLK)]).astype(jnp.int32)
    panel, energies_next, diagonal, neighbour = finish(
        at, sums, early[0], early[1], energies.reshape(1, n), lead_energy
    )
    return panel, energies_next.reshape(n), diagonal, neighbour


def solution(mesh):
    torus = Mesh(mesh.devices.reshape(8, 2, 4, 2, 2), ALL)
    in_specs = (P(BLK, PAR), P(BLK))
    out_specs = (P(BLK, None), P(BLK), P(ALL, None), P(ALL, None))
    return jax.shard_map(
        on_device, mesh=torus, in_specs=in_specs, out_specs=out_specs, check_vma=False
    )
```

```python
import functools

import jax
import jax.numpy as jnp
from jax import lax
from jax.experimental import pallas as pl
from jax.experimental.pallas import tpu as pltpu
from jax.sharding import Mesh
from jax.sharding import PartitionSpec as P


BLK = ("z", "xh", "y")
PLANE = ("xh", "y")
PAR = ("xl", "core")
ALL = BLK + PAR
HIGHEST = lax.Precision.HIGHEST


ridge_shift = 0.05
CHUNK = 64


def dot(a, b, ca, cb):
    return lax.dot_general(
        a, b, (((ca,), (cb,)), ((), ())), precision=HIGHEST, preferred_element_type=jnp.float32
    )


def outer_tile(left_rows, right_rows):
    return dot(left_rows, right_rows, 1, 1)


def unit(rows, columns):
    return lax.broadcasted_iota(jnp.int32, (rows, columns), 0) == lax.broadcasted_iota(
        jnp.int32, (rows, columns), 1
    )


def triangle_inverse(tile):
    n = tile.shape[0]
    held = jnp.concatenate([tile, unit(n, n).astype(jnp.float32)], axis=1)
    rows = lax.broadcasted_iota(jnp.int32, held.shape, 0)
    for j in range(0, n, 2):
        low = (j // 8) * 8
        part, at = held[low:, :], rows[low:]
        first = jnp.broadcast_to(part[:, j : j + 1], part.shape)
        second = jnp.broadcast_to(part[:, j + 1 : j + 2], part.shape)
        row_a, row_b = held[j : j + 1, :], held[j + 1 : j + 2, :]
        k = j - low
        a, b, c = first[k : k + 1], first[k + 1 : k + 2], second[k + 1 : k + 2]
        over_a = 1.0 / a
        over_det = 1.0 / (a * c - b * b)
        t = b * over_a
        row_b = row_b - t * row_a
        update = first * over_a * row_a + (second - first * t) * (a * over_det) * row_b
        update = jnp.where(at > j + 1, update, 0.0)
        update = jnp.where(at == j + 1, jnp.broadcast_to(t * row_a, part.shape), update)
        part = part - update
        held = jnp.concatenate([held[:low], part], axis=0) if low else part
    pivots = jnp.sum(jnp.where(unit(n, 2 * n), held, 0.0), axis=1, keepdims=True)
    return held[:, n:] * (1.0 / jnp.sqrt(pivots))


def eliminate(tile_ref, inverse_ref, first, last):
    n = tile_ref.shape[0]
    for r0 in range(first * CHUNK, last * CHUNK, CHUNK):
        r1 = r0 + CHUNK
        small = triangle_inverse(tile_ref[r0:r1, r0:r1])
        if r0:
            inverse_ref[r0:r1, :r0] = dot(small, inverse_ref[r0:r1, :r0], 1, 0)
        inverse_ref[r0:r1, r0:r1] = small
        if r1 < n:
            across = dot(small, tile_ref[r0:r1, r1:], 1, 0)
            tile_ref[r1:, r1:] = tile_ref[r1:, r1:] - dot(across, across, 0, 0)
            inverse_ref[r1:, :r1] = inverse_ref[r1:, :r1] - dot(
                across, inverse_ref[r0:r1, :r1], 0, 0
            )


def factor_first_kernel(sum_ref, tile_ref, inverse_ref):
    n = sum_ref.shape[0]
    tile_ref[...] = sum_ref[...] + ridge_shift * unit(n, n).astype(jnp.float32)
    inverse_ref[...] = jnp.zeros((n, n), jnp.float32)
    eliminate(tile_ref, inverse_ref, 0, n // CHUNK // 2)


def factor_second_kernel(at_ref, tile_in_ref, inverse_in_ref, energy_ref, packed_ref, tile_ref, inverse_ref):
    n = tile_ref.shape[0]
    share = n // 4
    tile_ref[...] = tile_in_ref[...]
    inverse_ref[...] = inverse_in_ref[...]
    eliminate(tile_ref, inverse_ref, n // CHUNK // 2, n // CHUNK)
    start = pl.multiple_of(at_ref[0] * share, share)
    packed_ref[:share, :] = inverse_ref[pl.ds(start, share), :]
    packed_ref[share:, :] = outer_tile(jnp.broadcast_to(energy_ref[...], (8, n)), inverse_ref[...])


VMEM = pl.BlockSpec(memory_space=pltpu.VMEM)
SMEM = pl.BlockSpec(memory_space=pltpu.SMEM)


def f32(*shape):
    return jax.ShapeDtypeStruct(shape, jnp.float32)


def cost(flops):
    return pl.CostEstimate(flops=flops, bytes_accessed=2**20, transcendentals=0)


def factor_first(total):
    n = total.shape[0]
    return pl.pallas_call(
        factor_first_kernel,
        out_shape=(f32(n, n), f32(n, n)),
        in_specs=[VMEM],
        out_specs=(VMEM,) * 2,
        name="factor_first",
        cost_estimate=cost(8 * 10**9),
    )(total)


def factor_second(at, tile, inverse, energies):
    n = tile.shape[0]
    return pl.pallas_call(
        factor_second_kernel,
        out_shape=f32(n // 4 + 8, n),
        in_specs=[SMEM] + [VMEM] * 3,
        out_specs=VMEM,
        scratch_shapes=[pltpu.VMEM((n, n), jnp.float32)] * 2,
        name="factor_second",
        cost_estimate=cost(8 * 10**9),
    )(at, tile, inverse, energies)


def cross_kernel(rows_ref, prev_ref, lead_ref, out_ref):
    out_ref[0] = outer_tile(rows_ref[...], lead_ref[...])
    out_ref[1] = outer_tile(prev_ref[...], lead_ref[...])


def cross(rows, prev_rows, lead_rows):
    n = rows.shape[0]
    return pl.pallas_call(
        cross_kernel,
        out_shape=f32(2, n, n),
        in_specs=[VMEM] * 3,
        out_specs=VMEM,
        name="cross",
        cost_estimate=cost(10**9),
    )(rows, prev_rows, lead_rows)


def finish_kernel(
    at_ref, own_ref, other_ref, self_ref, cycle_ref, energy_ref, a0_ref, a1_ref, b0_ref, b1_ref,
    panel_ref, energies_ref, diagonal_ref, neighbour_ref, sums_ref, inverse_ref, prev_ref,
):
    n = inverse_ref.shape[0]
    share, half = n // 4, n // 2
    par, core = at_ref[0], at_ref[2]
    for i, source in ((0, a0_ref), (2, a1_ref), (1, b0_ref), (3, b1_ref)):
        flip = jnp.bitwise_xor(par, i)
        inverse_ref[pl.ds(pl.multiple_of(flip * share, share), share), :] = source[:share, :]
    for i, source in ((0, own_ref), (1, other_ref)):
        start = pl.multiple_of(jnp.bitwise_xor(core, i) * half, half)
        sums_ref[0, pl.ds(start, half), :] = source[0]
        sums_ref[1, pl.ds(start, half), :] = source[1]
    inverse = inverse_ref[...]
    panel = outer_tile(sums_ref[0], inverse)
    panel_ref[...] = panel
    prev_ref[...] = outer_tile(sums_ref[1], inverse)
    start = pl.multiple_of(par * share, share)
    own = panel_ref[pl.ds(start, share), :]
    shifted = (
        lax.broadcasted_iota(jnp.int32, (share, n), 0) + start
        == lax.broadcasted_iota(jnp.int32, (share, n), 1)
    ).astype(jnp.float32)
    diagonal_ref[...] = (
        self_ref[pl.ds(start, share), :] + ridge_shift * shifted - outer_tile(own, panel)
    )
    neighbour_ref[...] = cycle_ref[...] - outer_tile(own, prev_ref[...])
    lead = a0_ref[share:, :]
    remainder = energy_ref[...] - outer_tile(lead, panel)[:1]
    energies_ref[...] = jnp.where(at_ref[1] == 0, lead[:1], remainder)


def finish(at, own, other, self_sum, cycle_rows, energies, parts):
    n = self_sum.shape[-1]
    share = n // 4
    return pl.pallas_call(
        finish_kernel,
        out_shape=(f32(n, n), f32(1, n), f32(share, n), f32(share, n)),
        in_specs=[SMEM] + [VMEM] * 9,
        out_specs=(VMEM,) * 4,
        scratch_shapes=[
            pltpu.VMEM((2, n, n), jnp.float32),
            pltpu.VMEM((n, n), jnp.float32),
            pltpu.VMEM((n, n), jnp.float32),
        ],
        name="finish",
        cost_estimate=cost(10**9),
    )(at, own, other, self_sum, cycle_rows, energies, *parts)


def swapped(value, axis):
    return lax.ppermute(value, axis, [(0, 1), (1, 0)])


def passed_along(block, axis, distance):
    count = lax.axis_size(axis)
    return lax.ppermute(block, axis, [((i - distance) % count, i) for i in range(count)])


def sum_scattered(partials):
    k, n = partials.shape[0], partials.shape[-1]
    quarters = partials.reshape(k, 2, 2, n // 4, n)
    core, xl = lax.axis_index("core"), lax.axis_index("xl")
    pick = lambda a, i, d: lax.dynamic_index_in_dim(a, i, d, keepdims=False)
    halves = pick(quarters, core, 2) + swapped(pick(quarters, 1 - core, 2), "core")
    return pick(halves, xl, 1) + swapped(pick(halves, 1 - xl, 1), "xl")


def sum_halves(partials):
    k, n = partials.shape[0], partials.shape[-1]
    core = lax.axis_index("core")
    chip = partials + swapped(partials, "core")
    halves = chip.reshape(k, 2, n // 2, n)
    own = lax.dynamic_index_in_dim(halves, core, 1, keepdims=False)
    own = own + swapped(own, "xl")
    return own, swapped(own, "core")


def total(values):
    return functools.reduce(jnp.add, values)


def scatter_lead(rows):
    parts = lax.axis_size(PLANE)
    part = rows.shape[0] // parts
    got = [lax.ppermute(rows[k * part : (k + 1) * part], BLK, [(0, k)]) for k in range(1, parts)]
    return jnp.where(lax.axis_index(PLANE) == 0, rows[:part], total(got))


def along_z(piece):
    got = [lax.ppermute(piece, "z", [(0, k)]) for k in range(1, lax.axis_size("z"))]
    return jnp.where(lax.axis_index("z") == 0, piece, total(got))


def over_plane(piece):
    parts = lax.axis_size(PLANE)
    copies = jnp.broadcast_to(piece, (parts, *piece.shape))
    return lax.all_to_all(copies, PLANE, split_axis=0, concat_axis=0, tiled=True)


def small_tree(value):
    z, xh, y = (lax.axis_index(a) for a in BLK)
    rounds = (
        ([[(0, 8 * k)] for k in (4, 2, 6)], z == 0),
        ([[(8 * k, 8 * k + d) for k in range(0, 8, 2)] for d in (4, 12, 8)], (z % 2 == 0) & (xh == 0)),
        ([[(4 * k, 4 * k + d) for k in range(16)] for d in (2, 1, 3)], y == 0),
    )
    for routes, holds in rounds:
        got = [lax.ppermute(value, BLK, route) for route in routes]
        value = jnp.where(holds, value, total(got))
    return value


def on_device(log_derivs, energies):
    n = log_derivs.shape[0]
    energy_row = energies.reshape(1, n)
    at = jnp.stack(
        [lax.axis_index(PAR), lax.axis_index(BLK), lax.axis_index("core")]
    ).astype(jnp.int32)
    piece = scatter_lead(log_derivs)
    prev_rows = passed_along(log_derivs, BLK, 1)
    own, other = sum_halves(outer_tile(log_derivs, log_derivs)[None])
    core = lax.axis_index("core")
    self_sum = jnp.concatenate(
        [jnp.where(core == 0, own[0], other[0]), jnp.where(core == 0, other[0], own[0])]
    )
    piece = along_z(piece)
    tile, inverse = factor_first(self_sum)
    lead_rows = over_plane(piece).reshape(log_derivs.shape)
    packed = factor_second(at, tile, inverse, energy_row)
    packed = small_tree(packed)
    across = swapped(packed, "xl")
    parts = (packed, across, swapped(packed, "core"), swapped(across, "core"))
    cycle_rows = sum_scattered(outer_tile(log_derivs, prev_rows)[None])[0]
    own, other = sum_halves(cross(log_derivs, prev_rows, lead_rows))
    panel, energies_next, diagonal, neighbour = finish(
        at, own, other, self_sum, cycle_rows, energy_row, parts
    )
    return panel, energies_next.reshape(n), diagonal, neighbour


def solution(mesh):
    torus = Mesh(mesh.devices.reshape(8, 2, 4, 2, 2), ALL)
    in_specs = (P(BLK, PAR), P(BLK))
    out_specs = (P(BLK, None), P(BLK), P(ALL, None), P(ALL, None))
    return jax.shard_map(
        on_device, mesh=torus, in_specs=in_specs, out_specs=out_specs, check_vma=False
    )
```

```python
import functools

import jax
import jax.numpy as jnp
from jax import lax
from jax.experimental import pallas as pl
from jax.experimental.pallas import tpu as pltpu
from jax.sharding import Mesh
from jax.sharding import PartitionSpec as P


BLK = ("zh", "zl", "xh", "y")
PLANE = ("zl", "y")
STACK = ("zh", "xh")
PAR = ("xl", "core")
ALL = BLK + PAR
HIGHEST = lax.Precision.HIGHEST


ridge_shift = 0.05
CHUNK = 64


def dot(a, b, ca, cb):
    return lax.dot_general(
        a, b, (((ca,), (cb,)), ((), ())), precision=HIGHEST, preferred_element_type=jnp.float32
    )


def outer_tile(left_rows, right_rows):
    return dot(left_rows, right_rows, 1, 1)


def unit(rows, columns):
    return lax.broadcasted_iota(jnp.int32, (rows, columns), 0) == lax.broadcasted_iota(
        jnp.int32, (rows, columns), 1
    )


def triangle_inverse(tile):
    n = tile.shape[0]
    held = jnp.concatenate([tile, unit(n, n).astype(jnp.float32)], axis=1)
    rows = lax.broadcasted_iota(jnp.int32, held.shape, 0)
    for j in range(0, n, 2):
        low = (j // 8) * 8
        part, at = held[low:, :], rows[low:]
        first = jnp.broadcast_to(part[:, j : j + 1], part.shape)
        second = jnp.broadcast_to(part[:, j + 1 : j + 2], part.shape)
        row_a, row_b = held[j : j + 1, :], held[j + 1 : j + 2, :]
        k = j - low
        a, b, c = first[k : k + 1], first[k + 1 : k + 2], second[k + 1 : k + 2]
        over_a = 1.0 / a
        over_det = 1.0 / (a * c - b * b)
        t = b * over_a
        row_b = row_b - t * row_a
        update = first * over_a * row_a + (second - first * t) * (a * over_det) * row_b
        update = jnp.where(at > j + 1, update, 0.0)
        update = jnp.where(at == j + 1, jnp.broadcast_to(t * row_a, part.shape), update)
        part = part - update
        held = jnp.concatenate([held[:low], part], axis=0) if low else part
    pivots = jnp.sum(jnp.where(unit(n, 2 * n), held, 0.0), axis=1, keepdims=True)
    return held[:, n:] * (1.0 / jnp.sqrt(pivots))


def eliminate(tile_ref, inverse_ref, first, last):
    n = tile_ref.shape[0]
    for r0 in range(first * CHUNK, last * CHUNK, CHUNK):
        r1 = r0 + CHUNK
        small = triangle_inverse(tile_ref[r0:r1, r0:r1])
        if r0:
            inverse_ref[r0:r1, :r0] = dot(small, inverse_ref[r0:r1, :r0], 1, 0)
        inverse_ref[r0:r1, r0:r1] = small
        if r1 < n:
            across = dot(small, tile_ref[r0:r1, r1:], 1, 0)
            tile_ref[r1:, r1:] = tile_ref[r1:, r1:] - dot(across, across, 0, 0)
            inverse_ref[r1:, :r1] = inverse_ref[r1:, :r1] - dot(
                across, inverse_ref[r0:r1, :r1], 0, 0
            )


def factor_first_kernel(sum_ref, tile_ref, inverse_ref):
    n = sum_ref.shape[0]
    tile_ref[...] = sum_ref[...] + ridge_shift * unit(n, n).astype(jnp.float32)
    inverse_ref[...] = jnp.zeros((n, n), jnp.float32)
    eliminate(tile_ref, inverse_ref, 0, n // CHUNK // 2)


def factor_second_kernel(at_ref, tile_in_ref, inverse_in_ref, energy_ref, packed_ref, tile_ref, inverse_ref):
    n = tile_ref.shape[0]
    share = n // 4
    tile_ref[...] = tile_in_ref[...]
    inverse_ref[...] = inverse_in_ref[...]
    eliminate(tile_ref, inverse_ref, n // CHUNK // 2, n // CHUNK)
    half = n // 2
    start = pl.multiple_of(at_ref[2] * share, share)
    packed_ref[:share, :] = inverse_ref[pl.ds(start, share), :half]
    packed_ref[share:half, :] = inverse_ref[pl.ds(start + half, share), :half]
    packed_ref[half : half + share, :] = inverse_ref[pl.ds(start + half, share), half:]
    lead = outer_tile(jnp.broadcast_to(energy_ref[...], (8, n)), inverse_ref[...])
    first = lax.broadcasted_iota(jnp.int32, (8, half), 0) == 0
    packed_ref[half + share :, :] = jnp.where(first, lead[:, :half], lead[:, half:])


VMEM = pl.BlockSpec(memory_space=pltpu.VMEM)
SMEM = pl.BlockSpec(memory_space=pltpu.SMEM)
GRANT = pltpu.CompilerParams(vmem_limit_bytes=16 * 2**20)


def f32(*shape):
    return jax.ShapeDtypeStruct(shape, jnp.float32)


def cost(flops):
    return pl.CostEstimate(flops=flops, bytes_accessed=2**20, transcendentals=0)


def factor_first(total):
    n = total.shape[0]
    return pl.pallas_call(
        factor_first_kernel,
        out_shape=(f32(n, n), f32(n, n)),
        in_specs=[VMEM],
        out_specs=(VMEM,) * 2,
        name="factor_first",
        compiler_params=GRANT,
        cost_estimate=cost(8 * 10**9),
    )(total)


def factor_second(at, tile, inverse, energies):
    n = tile.shape[0]
    return pl.pallas_call(
        factor_second_kernel,
        out_shape=f32(3 * n // 4 + 8, n // 2),
        in_specs=[SMEM] + [VMEM] * 3,
        out_specs=VMEM,
        scratch_shapes=[pltpu.VMEM((n, n), jnp.float32)] * 2,
        name="factor_second",
        compiler_params=GRANT,
        cost_estimate=cost(8 * 10**9),
    )(at, tile, inverse, energies)


def cross_kernel(rows_ref, prev_ref, lead_ref, out_ref):
    out_ref[0] = outer_tile(rows_ref[...], lead_ref[...])
    out_ref[1] = outer_tile(prev_ref[...], lead_ref[...])


def cross(rows, prev_rows, lead_rows):
    n = rows.shape[0]
    return pl.pallas_call(
        cross_kernel,
        out_shape=f32(2, n, n),
        in_specs=[VMEM] * 3,
        out_specs=VMEM,
        name="cross",
        compiler_params=GRANT,
        cost_estimate=cost(10**9),
    )(rows, prev_rows, lead_rows)


def finish_kernel(
    at_ref, own_ref, other_ref, self_ref, cycle_ref, energy_ref, mine_ref, twin_ref,
    panel_ref, energies_ref, diagonal_ref, neighbour_ref, sums_ref, inverse_ref, prev_ref,
):
    n = inverse_ref.shape[0]
    share, half = n // 4, n // 2
    par, core = at_ref[0], at_ref[2]
    inverse_ref[:half, half:] = jnp.zeros((half, half), jnp.float32)
    for i, source in ((0, mine_ref), (1, twin_ref)):
        start = pl.multiple_of(jnp.bitwise_xor(core, i) * share, share)
        inverse_ref[pl.ds(start, share), :half] = source[:share, :]
        inverse_ref[pl.ds(start + half, share), :half] = source[share:half, :]
        inverse_ref[pl.ds(start + half, share), half:] = source[half : half + share, :]
    for i, source in ((0, own_ref), (1, other_ref)):
        start = pl.multiple_of(jnp.bitwise_xor(core, i) * half, half)
        sums_ref[0, pl.ds(start, half), :] = source[0]
        sums_ref[1, pl.ds(start, half), :] = source[1]
    inverse = inverse_ref[...]
    panel = outer_tile(sums_ref[0], inverse)
    panel_ref[...] = panel
    prev_ref[...] = outer_tile(sums_ref[1], inverse)
    start = pl.multiple_of(par * share, share)
    own = panel_ref[pl.ds(start, share), :]
    shifted = (
        lax.broadcasted_iota(jnp.int32, (share, n), 0) + start
        == lax.broadcasted_iota(jnp.int32, (share, n), 1)
    ).astype(jnp.float32)
    diagonal_ref[...] = (
        self_ref[pl.ds(start, share), :] + ridge_shift * shifted - outer_tile(own, panel)
    )
    neighbour_ref[...] = cycle_ref[...] - outer_tile(own, prev_ref[...])
    last = half + share
    lead = jnp.concatenate([mine_ref[last : last + 1, :], mine_ref[last + 1 : last + 2, :]], axis=1)
    remainder = energy_ref[...] - outer_tile(jnp.broadcast_to(lead, (8, n)), panel)[:1]
    energies_ref[...] = jnp.where(at_ref[1] == 0, lead, remainder)


def finish(at, own, other, self_sum, cycle_rows, energies, parts):
    n = self_sum.shape[-1]
    share = n // 4
    return pl.pallas_call(
        finish_kernel,
        out_shape=(f32(n, n), f32(1, n), f32(share, n), f32(share, n)),
        in_specs=[SMEM] + [VMEM] * 7,
        out_specs=(VMEM,) * 4,
        scratch_shapes=[
            pltpu.VMEM((2, n, n), jnp.float32),
            pltpu.VMEM((n, n), jnp.float32),
            pltpu.VMEM((n, n), jnp.float32),
        ],
        name="finish",
        compiler_params=GRANT,
        cost_estimate=cost(10**9),
    )(at, own, other, self_sum, cycle_rows, energies, *parts)


def swapped(value, axis):
    return lax.ppermute(value, axis, [(0, 1), (1, 0)])


def passed_along(block, axis, distance):
    count = lax.axis_size(axis)
    return lax.ppermute(block, axis, [((i - distance) % count, i) for i in range(count)])


def sum_scattered(partials):
    k, n = partials.shape[0], partials.shape[-1]
    quarters = partials.reshape(k, 2, 2, n // 4, n)
    core, xl = lax.axis_index("core"), lax.axis_index("xl")
    pick = lambda a, i, d: lax.dynamic_index_in_dim(a, i, d, keepdims=False)
    halves = pick(quarters, core, 2) + swapped(pick(quarters, 1 - core, 2), "core")
    return pick(halves, xl, 1) + swapped(pick(halves, 1 - xl, 1), "xl")


def sum_halves(partials):
    k, n = partials.shape[0], partials.shape[-1]
    core = lax.axis_index("core")
    chip = partials + swapped(partials, "core")
    halves = chip.reshape(k, 2, n // 2, n)
    own = lax.dynamic_index_in_dim(halves, core, 1, keepdims=False)
    own = own + swapped(own, "xl")
    return own, swapped(own, "core")


SCATTER_ORDER = (6, 2, 5, 7, 1, 3, 4)
STACK_ORDER = (5, 4, 3, 7, 2, 6, 1)


def total(values):
    return functools.reduce(jnp.add, values)


def scatter_lead(rows):
    parts = lax.axis_size(PLANE)
    part = rows.shape[0] // parts
    got = [
        lax.ppermute(rows[k * part : (k + 1) * part], BLK, [(0, k // 4 * 8 + k % 4)])
        for k in SCATTER_ORDER
    ]
    return jnp.where(lax.axis_index(PLANE) == 0, rows[:part], total(got))


def along_stack(piece):
    got = [lax.ppermute(piece, STACK, [(0, k)]) for k in STACK_ORDER]
    return jnp.where(lax.axis_index(STACK) == 0, piece, total(got))


def over_plane(piece):
    parts = lax.axis_size(PLANE)
    copies = jnp.broadcast_to(piece, (parts, *piece.shape))
    return lax.all_to_all(copies, PLANE, split_axis=0, concat_axis=0, tiled=True)


def small_tree(value):
    zh, zl, xh, y = (lax.axis_index(a) for a in BLK)
    z = zh * 2 + zl
    rounds = (
        ([[(0, 8 * k)] for k in (4, 2, 6)], z == 0),
        ([[(8 * k, 8 * k + d) for k in range(0, 8, 2)] for d in (4, 12, 8)], (z % 2 == 0) & (xh == 0)),
        ([[(4 * k, 4 * k + d) for k in range(16)] for d in (2, 1, 3)], y == 0),
    )
    for routes, holds in rounds:
        got = [lax.ppermute(value, BLK, route) for route in routes]
        value = jnp.where(holds, value, total(got))
    return value


def on_device(log_derivs, energies):
    n = log_derivs.shape[0]
    energy_row = energies.reshape(1, n)
    at = jnp.stack(
        [lax.axis_index(PAR), lax.axis_index(BLK), lax.axis_index("core")]
    ).astype(jnp.int32)
    piece = scatter_lead(log_derivs)
    prev_rows = passed_along(log_derivs, BLK, 1)
    self_part = outer_tile(log_derivs, log_derivs)[None]
    own, other = sum_halves(self_part)
    upper = lax.axis_index("core") == 0
    self_sum = jnp.concatenate(
        [jnp.where(upper, own[0], other[0]), jnp.where(upper, other[0], own[0])]
    )
    piece = along_stack(piece)
    tile, inverse = factor_first(self_sum)
    lead_rows = over_plane(piece).reshape(log_derivs.shape)
    packed = factor_second(at, tile, inverse, energy_row)
    packed = small_tree(packed)
    twin = swapped(packed, "core")
    cycle_rows = sum_scattered(outer_tile(log_derivs, prev_rows)[None])[0]
    partials = cross(log_derivs, prev_rows, lead_rows)
    own, other = sum_halves(partials)
    panel, energies_next, diagonal, neighbour = finish(
        at, own, other, self_sum, cycle_rows, energy_row, (packed, twin)
    )
    return panel, energies_next.reshape(n), diagonal, neighbour


def solution(mesh):
    torus = Mesh(mesh.devices.reshape(4, 2, 2, 4, 2, 2), ALL)
    in_specs = (P(BLK, PAR), P(BLK))
    out_specs = (P(BLK, None), P(BLK), P(ALL, None), P(ALL, None))
    return jax.shard_map(
        on_device, mesh=torus, in_specs=in_specs, out_specs=out_specs, check_vma=False
    )
```

```python
import functools

import jax
import jax.numpy as jnp
from jax import lax
from jax.experimental import pallas as pl
from jax.experimental.pallas import tpu as pltpu
from jax.sharding import Mesh
from jax.sharding import PartitionSpec as P


BLK = ("z", "xh", "y")
PLANE = ("xh", "y")
PAR = ("xl", "core")
ALL = BLK + PAR
HIGHEST = lax.Precision.HIGHEST


ridge_shift = 0.05
CHUNK = 64


def dot(a, b, ca, cb):
    return lax.dot_general(
        a, b, (((ca,), (cb,)), ((), ())), precision=HIGHEST, preferred_element_type=jnp.float32
    )


def outer_tile(left_rows, right_rows):
    return dot(left_rows, right_rows, 1, 1)


def unit(rows, columns):
    return lax.broadcasted_iota(jnp.int32, (rows, columns), 0) == lax.broadcasted_iota(
        jnp.int32, (rows, columns), 1
    )


def triangle_inverse(tile):
    n = tile.shape[0]
    held = jnp.concatenate([tile, unit(n, n).astype(jnp.float32)], axis=1)
    rows = lax.broadcasted_iota(jnp.int32, held.shape, 0)
    for j in range(0, n, 2):
        low = (j // 8) * 8
        part, at = held[low:, :], rows[low:]
        first = jnp.broadcast_to(part[:, j : j + 1], part.shape)
        second = jnp.broadcast_to(part[:, j + 1 : j + 2], part.shape)
        row_a, row_b = held[j : j + 1, :], held[j + 1 : j + 2, :]
        k = j - low
        a, b, c = first[k : k + 1], first[k + 1 : k + 2], second[k + 1 : k + 2]
        over_a = 1.0 / a
        over_det = 1.0 / (a * c - b * b)
        t = b * over_a
        row_b = row_b - t * row_a
        update = first * over_a * row_a + (second - first * t) * (a * over_det) * row_b
        update = jnp.where(at > j + 1, update, 0.0)
        update = jnp.where(at == j + 1, jnp.broadcast_to(t * row_a, part.shape), update)
        part = part - update
        held = jnp.concatenate([held[:low], part], axis=0) if low else part
    pivots = jnp.sum(jnp.where(unit(n, 2 * n), held, 0.0), axis=1, keepdims=True)
    return held[:, n:] * (1.0 / jnp.sqrt(pivots))


def eliminate(tile_ref, inverse_ref, first, last):
    n = tile_ref.shape[0]
    for r0 in range(first * CHUNK, last * CHUNK, CHUNK):
        r1 = r0 + CHUNK
        small = triangle_inverse(tile_ref[r0:r1, r0:r1])
        if r0:
            inverse_ref[r0:r1, :r0] = dot(small, inverse_ref[r0:r1, :r0], 1, 0)
        inverse_ref[r0:r1, r0:r1] = small
        if r1 < n:
            across = dot(small, tile_ref[r0:r1, r1:], 1, 0)
            tile_ref[r1:, r1:] = tile_ref[r1:, r1:] - dot(across, across, 0, 0)
            inverse_ref[r1:, :r1] = inverse_ref[r1:, :r1] - dot(
                across, inverse_ref[r0:r1, :r1], 0, 0
            )


def factor_first_kernel(sum_ref, state_ref):
    n = sum_ref.shape[0]
    tile_ref, inverse_ref = state_ref.at[0], state_ref.at[1]
    tile_ref[...] = sum_ref[...] + ridge_shift * unit(n, n).astype(jnp.float32)
    inverse_ref[...] = jnp.zeros((n, n), jnp.float32)
    eliminate(tile_ref, inverse_ref, 0, n // CHUNK // 2)


def factor_second_kernel(at_ref, state_ref, energy_ref, packed_ref):
    n = state_ref.shape[-1]
    share = n // 4
    tile_ref, inverse_ref = state_ref.at[0], state_ref.at[1]
    eliminate(tile_ref, inverse_ref, n // CHUNK // 2, n // CHUNK)
    half = n // 2
    start = pl.multiple_of(at_ref[2] * share, share)
    packed_ref[:share, :] = inverse_ref[pl.ds(start, share), :half]
    packed_ref[share:half, :] = inverse_ref[pl.ds(start + half, share), :half]
    packed_ref[half : half + share, :] = inverse_ref[pl.ds(start + half, share), half:]
    lead = outer_tile(jnp.broadcast_to(energy_ref[...], (8, n)), inverse_ref[...])
    first = lax.broadcasted_iota(jnp.int32, (8, half), 0) == 0
    packed_ref[half + share :, :] = jnp.where(first, lead[:, :half], lead[:, half:])


VMEM = pl.BlockSpec(memory_space=pltpu.VMEM)
SMEM = pl.BlockSpec(memory_space=pltpu.SMEM)
GRANT = pltpu.CompilerParams(vmem_limit_bytes=16 * 2**20)


def f32(*shape):
    return jax.ShapeDtypeStruct(shape, jnp.float32)


def cost(flops):
    return pl.CostEstimate(flops=flops, bytes_accessed=2**20, transcendentals=0)


def factor_first(total):
    n = total.shape[0]
    return pl.pallas_call(
        factor_first_kernel,
        out_shape=f32(2, n, n),
        in_specs=[VMEM],
        out_specs=VMEM,
        name="factor_first",
        compiler_params=GRANT,
        cost_estimate=cost(8 * 10**9),
    )(total)


def factor_second(at, state, energies):
    n = state.shape[-1]

    def kernel(at_ref, state_in_ref, energy_ref, packed_ref, state_ref):
        state_ref[...] = state_in_ref[...]
        factor_second_kernel(at_ref, state_ref, energy_ref, packed_ref)

    return pl.pallas_call(
        kernel,
        out_shape=f32(3 * n // 4 + 8, n // 2),
        in_specs=[SMEM] + [VMEM] * 2,
        out_specs=VMEM,
        scratch_shapes=[pltpu.VMEM((2, n, n), jnp.float32)],
        name="factor_second",
        compiler_params=GRANT,
        cost_estimate=cost(8 * 10**9),
    )(at, state, energies)


def cross_kernel(rows_ref, prev_ref, lead_ref, out_ref):
    out_ref[0] = outer_tile(rows_ref[...], lead_ref[...])
    out_ref[1] = outer_tile(prev_ref[...], lead_ref[...])


def cross(rows, prev_rows, lead_rows):
    n = rows.shape[0]
    return pl.pallas_call(
        cross_kernel,
        out_shape=f32(2, n, n),
        in_specs=[VMEM] * 3,
        out_specs=VMEM,
        name="cross",
        compiler_params=GRANT,
        cost_estimate=cost(10**9),
    )(rows, prev_rows, lead_rows)


def finish_kernel(
    at_ref, own_ref, other_ref, self_ref, cycle_ref, energy_ref, mine_ref, twin_ref,
    panel_ref, energies_ref, diagonal_ref, neighbour_ref, sums_ref, inverse_ref, prev_ref,
):
    n = inverse_ref.shape[0]
    share, half = n // 4, n // 2
    par, core = at_ref[0], at_ref[2]
    inverse_ref[:half, half:] = jnp.zeros((half, half), jnp.float32)
    for i, source in ((0, mine_ref), (1, twin_ref)):
        start = pl.multiple_of(jnp.bitwise_xor(core, i) * share, share)
        inverse_ref[pl.ds(start, share), :half] = source[:share, :]
        inverse_ref[pl.ds(start + half, share), :half] = source[share:half, :]
        inverse_ref[pl.ds(start + half, share), half:] = source[half : half + share, :]
    for i, source in ((0, own_ref), (1, other_ref)):
        start = pl.multiple_of(jnp.bitwise_xor(core, i) * half, half)
        sums_ref[0, pl.ds(start, half), :] = source[0]
        sums_ref[1, pl.ds(start, half), :] = source[1]
    inverse = inverse_ref[...]
    panel = outer_tile(sums_ref[0], inverse)
    panel_ref[...] = panel
    prev_ref[...] = outer_tile(sums_ref[1], inverse)
    start = pl.multiple_of(par * share, share)
    own = panel_ref[pl.ds(start, share), :]
    shifted = (
        lax.broadcasted_iota(jnp.int32, (share, n), 0) + start
        == lax.broadcasted_iota(jnp.int32, (share, n), 1)
    ).astype(jnp.float32)
    diagonal_ref[...] = (
        self_ref[pl.ds(start, share), :] + ridge_shift * shifted - outer_tile(own, panel)
    )
    neighbour_ref[...] = cycle_ref[...] - outer_tile(own, prev_ref[...])
    last = half + share
    lead = jnp.concatenate([mine_ref[last : last + 1, :], mine_ref[last + 1 : last + 2, :]], axis=1)
    remainder = energy_ref[...] - outer_tile(jnp.broadcast_to(lead, (8, n)), panel)[:1]
    energies_ref[...] = jnp.where(at_ref[1] == 0, lead, remainder)


def finish(at, own, other, self_sum, cycle_rows, energies, parts):
    n = self_sum.shape[-1]
    share = n // 4
    return pl.pallas_call(
        finish_kernel,
        out_shape=(f32(n, n), f32(1, n), f32(share, n), f32(share, n)),
        in_specs=[SMEM] + [VMEM] * 7,
        out_specs=(VMEM,) * 4,
        scratch_shapes=[
            pltpu.VMEM((2, n, n), jnp.float32),
            pltpu.VMEM((n, n), jnp.float32),
            pltpu.VMEM((n, n), jnp.float32),
        ],
        name="finish",
        compiler_params=GRANT,
        cost_estimate=cost(10**9),
    )(at, own, other, self_sum, cycle_rows, energies, *parts)


def swapped(value, axis):
    return lax.ppermute(value, axis, [(0, 1), (1, 0)])


def passed_along(block, axis, distance):
    count = lax.axis_size(axis)
    return lax.ppermute(block, axis, [((i - distance) % count, i) for i in range(count)])


def sum_scattered(partials):
    k, n = partials.shape[0], partials.shape[-1]
    quarters = partials.reshape(k, 2, 2, n // 4, n)
    core, xl = lax.axis_index("core"), lax.axis_index("xl")
    pick = lambda a, i, d: lax.dynamic_index_in_dim(a, i, d, keepdims=False)
    halves = pick(quarters, core, 2) + swapped(pick(quarters, 1 - core, 2), "core")
    return pick(halves, xl, 1) + swapped(pick(halves, 1 - xl, 1), "xl")


def sum_halves(partials):
    k, n = partials.shape[0], partials.shape[-1]
    core = lax.axis_index("core")
    chip = partials + swapped(partials, "core")
    halves = chip.reshape(k, 2, n // 2, n)
    own = lax.dynamic_index_in_dim(halves, core, 1, keepdims=False)
    own = own + swapped(own, "xl")
    return own, swapped(own, "core")


SCATTER_ORDER = (6, 2, 5, 7, 1, 3, 4)
STACK_ORDER = (4, 3, 5, 2, 6, 1, 7)


def total(values):
    return functools.reduce(jnp.add, values)


def scatter_lead(rows):
    parts = lax.axis_size(PLANE)
    part = rows.shape[0] // parts
    got = [
        lax.ppermute(rows[k * part : (k + 1) * part], BLK, [(0, k)])
        for k in SCATTER_ORDER
    ]
    return jnp.where(lax.axis_index(PLANE) == 0, rows[:part], total(got))


def along_z(piece):
    got = [lax.ppermute(piece, "z", [(0, k)]) for k in STACK_ORDER]
    return jnp.where(lax.axis_index("z") == 0, piece, total(got))


def over_plane(piece):
    parts = lax.axis_size(PLANE)
    copies = jnp.broadcast_to(piece, (parts, *piece.shape))
    return lax.all_to_all(copies, PLANE, split_axis=0, concat_axis=0, tiled=True)


def small_tree(value):
    z, xh, y = (lax.axis_index(a) for a in BLK)
    rounds = (
        ([[(0, 8 * k)] for k in (4, 2, 6)], z == 0),
        ([[(8 * k, 8 * k + d) for k in range(0, 8, 2)] for d in (4, 12, 8)], (z % 2 == 0) & (xh == 0)),
        ([[(4 * k, 4 * k + d) for k in range(16)] for d in (2, 1, 3)], y == 0),
    )
    for routes, holds in rounds:
        got = [lax.ppermute(value, BLK, route) for route in routes]
        value = jnp.where(holds, value, total(got))
    return value


def on_device(log_derivs, energies):
    n = log_derivs.shape[0]
    energy_row = energies.reshape(1, n)
    at = jnp.stack(
        [lax.axis_index(PAR), lax.axis_index(BLK), lax.axis_index("core")]
    ).astype(jnp.int32)
    piece = scatter_lead(log_derivs)
    prev_rows = passed_along(log_derivs, BLK, 1)
    self_part = outer_tile(log_derivs, log_derivs)[None]
    own, other = sum_halves(self_part)
    upper = lax.axis_index("core") == 0
    self_sum = jnp.concatenate(
        [jnp.where(upper, own[0], other[0]), jnp.where(upper, other[0], own[0])]
    )
    piece = along_z(piece)
    state = factor_first(self_sum)
    lead_rows = over_plane(piece).reshape(log_derivs.shape)
    packed = factor_second(at, state, energy_row)
    packed = small_tree(packed)
    twin = swapped(packed, "core")
    cycle_rows = sum_scattered(outer_tile(log_derivs, prev_rows)[None])[0]
    partials = cross(log_derivs, prev_rows, lead_rows)
    own, other = sum_halves(partials)
    panel, energies_next, diagonal, neighbour = finish(
        at, own, other, self_sum, cycle_rows, energy_row, (packed, twin)
    )
    return panel, energies_next.reshape(n), diagonal, neighbour


def solution(mesh):
    torus = Mesh(mesh.devices.reshape(8, 2, 4, 2, 2), ALL)
    in_specs = (P(BLK, PAR), P(BLK))
    out_specs = (P(BLK, None), P(BLK), P(ALL, None), P(ALL, None))
    return jax.shard_map(
        on_device, mesh=torus, in_specs=in_specs, out_specs=out_specs, check_vma=False
    )
```

```python
import functools

import jax
import jax.numpy as jnp
from jax import lax
from jax.experimental import pallas as pl
from jax.experimental.pallas import tpu as pltpu
from jax.sharding import Mesh
from jax.sharding import PartitionSpec as P


BLK = ("z", "xh", "y")
PLANE = ("xh", "y")
PAR = ("xl", "core")
ALL = BLK + PAR
HIGHEST = lax.Precision.HIGHEST


ridge_shift = 0.05
CHUNK = 64


def dot(a, b, ca, cb):
    return lax.dot_general(
        a, b, (((ca,), (cb,)), ((), ())), precision=HIGHEST, preferred_element_type=jnp.float32
    )


def outer_tile(left_rows, right_rows):
    return dot(left_rows, right_rows, 1, 1)


def unit(rows, columns):
    return lax.broadcasted_iota(jnp.int32, (rows, columns), 0) == lax.broadcasted_iota(
        jnp.int32, (rows, columns), 1
    )


def triangle_inverse(tile):
    n = tile.shape[0]
    held = jnp.concatenate([tile, unit(n, n).astype(jnp.float32)], axis=1)
    rows = lax.broadcasted_iota(jnp.int32, held.shape, 0)
    for j in range(0, n, 2):
        low = (j // 8) * 8
        part, at = held[low:, :], rows[low:]
        first = jnp.broadcast_to(part[:, j : j + 1], part.shape)
        second = jnp.broadcast_to(part[:, j + 1 : j + 2], part.shape)
        row_a, row_b = held[j : j + 1, :], held[j + 1 : j + 2, :]
        k = j - low
        a, b, c = first[k : k + 1], first[k + 1 : k + 2], second[k + 1 : k + 2]
        over_a = 1.0 / a
        over_det = 1.0 / (a * c - b * b)
        t = b * over_a
        row_b = row_b - t * row_a
        update = first * over_a * row_a + (second - first * t) * (a * over_det) * row_b
        update = jnp.where(at > j + 1, update, 0.0)
        update = jnp.where(at == j + 1, jnp.broadcast_to(t * row_a, part.shape), update)
        part = part - update
        held = jnp.concatenate([held[:low], part], axis=0) if low else part
    pivots = jnp.sum(jnp.where(unit(n, 2 * n), held, 0.0), axis=1, keepdims=True)
    return held[:, n:] * (1.0 / jnp.sqrt(pivots))


def eliminate(tile_ref, inverse_ref, first, last):
    n = tile_ref.shape[0]
    for r0 in range(first * CHUNK, last * CHUNK, CHUNK):
        r1 = r0 + CHUNK
        small = triangle_inverse(tile_ref[r0:r1, r0:r1])
        if r0:
            inverse_ref[r0:r1, :r0] = dot(small, inverse_ref[r0:r1, :r0], 1, 0)
        inverse_ref[r0:r1, r0:r1] = small
        if r1 < n:
            across = dot(small, tile_ref[r0:r1, r1:], 1, 0)
            tile_ref[r1:, r1:] = tile_ref[r1:, r1:] - dot(across, across, 0, 0)
            inverse_ref[r1:, :r1] = inverse_ref[r1:, :r1] - dot(
                across, inverse_ref[r0:r1, :r1], 0, 0
            )


def factor_first_kernel(sum_ref, state_ref):
    n = sum_ref.shape[0]
    tile_ref, inverse_ref = state_ref.at[0], state_ref.at[1]
    tile_ref[...] = sum_ref[...] + ridge_shift * unit(n, n).astype(jnp.float32)
    inverse_ref[...] = jnp.zeros((n, n), jnp.float32)
    eliminate(tile_ref, inverse_ref, 0, n // CHUNK // 2)


def factor_second_kernel(at_ref, state_ref, energy_ref, packed_ref):
    n = state_ref.shape[-1]
    share = n // 4
    tile_ref, inverse_ref = state_ref.at[0], state_ref.at[1]
    eliminate(tile_ref, inverse_ref, n // CHUNK // 2, n // CHUNK)
    half = n // 2
    start = pl.multiple_of(at_ref[2] * share, share)
    packed_ref[:share, :] = inverse_ref[pl.ds(start, share), :half]
    packed_ref[share:half, :] = inverse_ref[pl.ds(start + half, share), :half]
    packed_ref[half : half + share, :] = inverse_ref[pl.ds(start + half, share), half:]
    lead = outer_tile(jnp.broadcast_to(energy_ref[...], (8, n)), inverse_ref[...])
    first = lax.broadcasted_iota(jnp.int32, (8, half), 0) == 0
    packed_ref[half + share :, :] = jnp.where(first, lead[:, :half], lead[:, half:])


VMEM = pl.BlockSpec(memory_space=pltpu.VMEM)
SMEM = pl.BlockSpec(memory_space=pltpu.SMEM)
GRANT = pltpu.CompilerParams(vmem_limit_bytes=16 * 2**20)


def f32(*shape):
    return jax.ShapeDtypeStruct(shape, jnp.float32)


def cost(flops):
    return pl.CostEstimate(flops=flops, bytes_accessed=2**20, transcendentals=0)


def factor_first(total):
    n = total.shape[0]
    return pl.pallas_call(
        factor_first_kernel,
        out_shape=f32(2, n, n),
        in_specs=[VMEM],
        out_specs=VMEM,
        name="factor_first",
        compiler_params=GRANT,
        cost_estimate=cost(8 * 10**9),
    )(total)


def factor_second(at, state, energies):
    n = state.shape[-1]

    def kernel(at_ref, state_in_ref, energy_ref, packed_ref, state_ref):
        state_ref[...] = state_in_ref[...]
        factor_second_kernel(at_ref, state_ref, energy_ref, packed_ref)

    return pl.pallas_call(
        kernel,
        out_shape=f32(3 * n // 4 + 8, n // 2),
        in_specs=[SMEM] + [VMEM] * 2,
        out_specs=VMEM,
        scratch_shapes=[pltpu.VMEM((2, n, n), jnp.float32)],
        name="factor_second",
        compiler_params=GRANT,
        cost_estimate=cost(8 * 10**9),
    )(at, state, energies)


def cross_kernel(rows_ref, prev_ref, lead_ref, out_ref):
    out_ref[0] = outer_tile(rows_ref[...], lead_ref[...])
    out_ref[1] = outer_tile(prev_ref[...], lead_ref[...])


def cross(rows, prev_rows, lead_rows):
    n = rows.shape[0]
    return pl.pallas_call(
        cross_kernel,
        out_shape=f32(2, n, n),
        in_specs=[VMEM] * 3,
        out_specs=VMEM,
        name="cross",
        compiler_params=GRANT,
        cost_estimate=cost(10**9),
    )(rows, prev_rows, lead_rows)


def finish_kernel(
    at_ref, own_ref, other_ref, self_ref, cycle_ref, energy_ref, mine_ref, twin_ref,
    panel_ref, energies_ref, diagonal_ref, neighbour_ref, sums_ref, inverse_ref, prev_ref,
):
    n = inverse_ref.shape[0]
    share, half = n // 4, n // 2
    par, core = at_ref[0], at_ref[2]
    inverse_ref[:half, half:] = jnp.zeros((half, half), jnp.float32)
    for i, source in ((0, mine_ref), (1, twin_ref)):
        start = pl.multiple_of(jnp.bitwise_xor(core, i) * share, share)
        inverse_ref[pl.ds(start, share), :half] = source[:share, :]
        inverse_ref[pl.ds(start + half, share), :half] = source[share:half, :]
        inverse_ref[pl.ds(start + half, share), half:] = source[half : half + share, :]
    for i, source in ((0, own_ref), (1, other_ref)):
        start = pl.multiple_of(jnp.bitwise_xor(core, i) * half, half)
        sums_ref[0, pl.ds(start, half), :] = source[0]
        sums_ref[1, pl.ds(start, half), :] = source[1]
    inverse = inverse_ref[...]
    panel = outer_tile(sums_ref[0], inverse)
    panel_ref[...] = panel
    prev_ref[...] = outer_tile(sums_ref[1], inverse)
    start = pl.multiple_of(par * share, share)
    own = panel_ref[pl.ds(start, share), :]
    shifted = (
        lax.broadcasted_iota(jnp.int32, (share, n), 0) + start
        == lax.broadcasted_iota(jnp.int32, (share, n), 1)
    ).astype(jnp.float32)
    diagonal_ref[...] = (
        self_ref[pl.ds(start, share), :] + ridge_shift * shifted - outer_tile(own, panel)
    )
    neighbour_ref[...] = cycle_ref[...] - outer_tile(own, prev_ref[...])
    last = half + share
    lead = jnp.concatenate([mine_ref[last : last + 1, :], mine_ref[last + 1 : last + 2, :]], axis=1)
    remainder = energy_ref[...] - outer_tile(jnp.broadcast_to(lead, (8, n)), panel)[:1]
    energies_ref[...] = jnp.where(at_ref[1] == 0, lead, remainder)


def finish(at, own, other, self_sum, cycle_rows, energies, parts):
    n = self_sum.shape[-1]
    share = n // 4
    return pl.pallas_call(
        finish_kernel,
        out_shape=(f32(n, n), f32(1, n), f32(share, n), f32(share, n)),
        in_specs=[SMEM] + [VMEM] * 7,
        out_specs=(VMEM,) * 4,
        scratch_shapes=[
            pltpu.VMEM((2, n, n), jnp.float32),
            pltpu.VMEM((n, n), jnp.float32),
            pltpu.VMEM((n, n), jnp.float32),
        ],
        name="finish",
        compiler_params=GRANT,
        cost_estimate=cost(10**9),
    )(at, own, other, self_sum, cycle_rows, energies, *parts)


def swapped(value, axis):
    return lax.ppermute(value, axis, [(0, 1), (1, 0)])


def sum_scattered(partials):
    k, n = partials.shape[0], partials.shape[-1]
    quarters = partials.reshape(k, 2, 2, n // 4, n)
    core, xl = lax.axis_index("core"), lax.axis_index("xl")
    pick = lambda a, i, d: lax.dynamic_index_in_dim(a, i, d, keepdims=False)
    halves = pick(quarters, core, 2) + swapped(pick(quarters, 1 - core, 2), "core")
    return pick(halves, xl, 1) + swapped(pick(halves, 1 - xl, 1), "xl")


def sum_halves(partials):
    k, n = partials.shape[0], partials.shape[-1]
    core = lax.axis_index("core")
    chip = partials + swapped(partials, "core")
    halves = chip.reshape(k, 2, n // 2, n)
    own = lax.dynamic_index_in_dim(halves, core, 1, keepdims=False)
    own = own + swapped(own, "xl")
    return own, swapped(own, "core")


SCATTER_ORDER = (6, 2, 5, 7, 1, 3, 4)
STACK_ORDER = (4, 3, 5, 2, 6, 1, 7)


def total(values):
    return functools.reduce(jnp.add, values)


def scatter_lead(rows):
    parts = lax.axis_size(PLANE)
    part = rows.shape[0] // parts
    got = [
        lax.ppermute(rows[k * part : (k + 1) * part], BLK, [(0, k)])
        for k in SCATTER_ORDER
    ]
    return jnp.where(lax.axis_index(PLANE) == 0, rows[:part], total(got))


def along_z(piece):
    got = [lax.ppermute(piece, "z", [(0, k)]) for k in STACK_ORDER]
    return jnp.where(lax.axis_index("z") == 0, piece, total(got))


def over_plane(piece):
    parts = lax.axis_size(PLANE)
    copies = jnp.broadcast_to(piece, (parts, *piece.shape))
    return lax.all_to_all(copies, PLANE, split_axis=0, concat_axis=0, tiled=True)


def small_tree(value):
    z, xh, y = (lax.axis_index(a) for a in BLK)
    rounds = (
        ([[(0, 8 * k)] for k in (4, 2, 6)], z == 0),
        ([[(8 * k, 8 * k + d) for k in range(0, 8, 2)] for d in (4, 12, 8)], (z % 2 == 0) & (xh == 0)),
        ([[(4 * k, 4 * k + d) for k in range(16)] for d in (2, 1, 3)], y == 0),
    )
    for routes, holds in rounds:
        got = [lax.ppermute(value, BLK, route) for route in routes]
        value = jnp.where(holds, value, total(got))
    return value


def on_device(log_derivs, energies):
    n = log_derivs.shape[0]
    energy_row = energies.reshape(1, n)
    at = jnp.stack(
        [lax.axis_index(PAR), lax.axis_index(BLK), lax.axis_index("core")]
    ).astype(jnp.int32)
    wrapped = lax.ppermute(log_derivs, BLK, [(b, (b + 1) % 64) for b in range(7, 64, 8)])
    piece = scatter_lead(log_derivs)
    near = lax.ppermute(log_derivs, BLK, [(b, b + 1) for b in range(64) if b % 8 != 7])
    prev_rows = jnp.where(lax.axis_index(PLANE) == 0, wrapped, near)
    self_part = outer_tile(log_derivs, log_derivs)[None]
    own, other = sum_halves(self_part)
    upper = lax.axis_index("core") == 0
    self_sum = jnp.concatenate(
        [jnp.where(upper, own[0], other[0]), jnp.where(upper, other[0], own[0])]
    )
    piece = along_z(piece)
    state = factor_first(self_sum)
    lead_rows = over_plane(piece).reshape(log_derivs.shape)
    packed = factor_second(at, state, energy_row)
    packed = small_tree(packed)
    twin = swapped(packed, "core")
    cycle_rows = sum_scattered(outer_tile(log_derivs, prev_rows)[None])[0]
    partials = cross(log_derivs, prev_rows, lead_rows)
    own, other = sum_halves(partials)
    panel, energies_next, diagonal, neighbour = finish(
        at, own, other, self_sum, cycle_rows, energy_row, (packed, twin)
    )
    return panel, energies_next.reshape(n), diagonal, neighbour


def solution(mesh):
    torus = Mesh(mesh.devices.reshape(8, 2, 4, 2, 2), ALL)
    in_specs = (P(BLK, PAR), P(BLK))
    out_specs = (P(BLK, None), P(BLK), P(ALL, None), P(ALL, None))
    return jax.shard_map(
        on_device, mesh=torus, in_specs=in_specs, out_specs=out_specs, check_vma=False
    )
```

```python
import functools

import jax
import jax.numpy as jnp
from jax import lax
from jax.experimental import pallas as pl
from jax.experimental.pallas import tpu as pltpu
from jax.sharding import Mesh
from jax.sharding import PartitionSpec as P


BLK = ("z", "xh", "y")
PLANE = ("xh", "y")
PAR = ("xl", "core")
ALL = BLK + PAR
HIGHEST = lax.Precision.HIGHEST


ridge_shift = 0.05
CHUNK = 64


def dot(a, b, ca, cb):
    return lax.dot_general(
        a, b, (((ca,), (cb,)), ((), ())), precision=HIGHEST, preferred_element_type=jnp.float32
    )


def outer_tile(left_rows, right_rows):
    return dot(left_rows, right_rows, 1, 1)


def unit(rows, columns):
    return lax.broadcasted_iota(jnp.int32, (rows, columns), 0) == lax.broadcasted_iota(
        jnp.int32, (rows, columns), 1
    )


def triangle_inverse(tile):
    n = tile.shape[0]
    held = jnp.concatenate([tile, unit(n, n).astype(jnp.float32)], axis=1)
    rows = lax.broadcasted_iota(jnp.int32, held.shape, 0)
    for j in range(0, n, 2):
        low = (j // 8) * 8
        part, at = held[low:, :], rows[low:]
        first = jnp.broadcast_to(part[:, j : j + 1], part.shape)
        second = jnp.broadcast_to(part[:, j + 1 : j + 2], part.shape)
        row_a, row_b = held[j : j + 1, :], held[j + 1 : j + 2, :]
        k = j - low
        a, b, c = first[k : k + 1], first[k + 1 : k + 2], second[k + 1 : k + 2]
        over_a = 1.0 / a
        over_det = 1.0 / (a * c - b * b)
        t = b * over_a
        row_b = row_b - t * row_a
        update = first * over_a * row_a + (second - first * t) * (a * over_det) * row_b
        update = jnp.where(at > j + 1, update, 0.0)
        update = jnp.where(at == j + 1, jnp.broadcast_to(t * row_a, part.shape), update)
        part = part - update
        held = jnp.concatenate([held[:low], part], axis=0) if low else part
    pivots = jnp.sum(jnp.where(unit(n, 2 * n), held, 0.0), axis=1, keepdims=True)
    return held[:, n:] * (1.0 / jnp.sqrt(pivots))


def eliminate(tile_ref, inverse_ref, first, last):
    n = tile_ref.shape[0]
    for r0 in range(first * CHUNK, last * CHUNK, CHUNK):
        r1 = r0 + CHUNK
        small = triangle_inverse(tile_ref[r0:r1, r0:r1])
        if r0:
            inverse_ref[r0:r1, :r0] = dot(small, inverse_ref[r0:r1, :r0], 1, 0)
        inverse_ref[r0:r1, r0:r1] = small
        if r1 < n:
            across = dot(small, tile_ref[r0:r1, r1:], 1, 0)
            tile_ref[r1:, r1:] = tile_ref[r1:, r1:] - dot(across, across, 0, 0)
            inverse_ref[r1:, :r1] = inverse_ref[r1:, :r1] - dot(
                across, inverse_ref[r0:r1, :r1], 0, 0
            )


def factor_first_kernel(sum_ref, state_ref):
    n = sum_ref.shape[0]
    tile_ref, inverse_ref = state_ref.at[0], state_ref.at[1]
    tile_ref[...] = sum_ref[...] + ridge_shift * unit(n, n).astype(jnp.float32)
    inverse_ref[...] = jnp.zeros((n, n), jnp.float32)
    eliminate(tile_ref, inverse_ref, 0, n // CHUNK // 2)


def factor_second_kernel(at_ref, state_ref, energy_ref, packed_ref):
    n = state_ref.shape[-1]
    share = n // 4
    tile_ref, inverse_ref = state_ref.at[0], state_ref.at[1]
    eliminate(tile_ref, inverse_ref, n // CHUNK // 2, n // CHUNK)
    half = n // 2
    start = pl.multiple_of(at_ref[2] * share, share)
    packed_ref[:share, :] = inverse_ref[pl.ds(start, share), :half]
    packed_ref[share:half, :] = inverse_ref[pl.ds(start + half, share), :half]
    packed_ref[half : half + share, :] = inverse_ref[pl.ds(start + half, share), half:]
    lead = outer_tile(jnp.broadcast_to(energy_ref[...], (8, n)), inverse_ref[...])
    first = lax.broadcasted_iota(jnp.int32, (8, half), 0) == 0
    packed_ref[half + share :, :] = jnp.where(first, lead[:, :half], lead[:, half:])


VMEM = pl.BlockSpec(memory_space=pltpu.VMEM)
SMEM = pl.BlockSpec(memory_space=pltpu.SMEM)
GRANT = pltpu.CompilerParams(vmem_limit_bytes=16 * 2**20)


def f32(*shape):
    return jax.ShapeDtypeStruct(shape, jnp.float32)


def cost(flops):
    return pl.CostEstimate(flops=flops, bytes_accessed=2**20, transcendentals=0)


def factor_first(total):
    n = total.shape[0]
    return pl.pallas_call(
        factor_first_kernel,
        out_shape=f32(2, n, n),
        in_specs=[VMEM],
        out_specs=VMEM,
        name="factor_first",
        compiler_params=GRANT,
        cost_estimate=cost(8 * 10**9),
    )(total)


def factor_second(at, state, energies):
    n = state.shape[-1]

    def kernel(at_ref, state_in_ref, energy_ref, packed_ref, state_ref):
        state_ref[...] = state_in_ref[...]
        factor_second_kernel(at_ref, state_ref, energy_ref, packed_ref)

    return pl.pallas_call(
        kernel,
        out_shape=f32(3 * n // 4 + 8, n // 2),
        in_specs=[SMEM] + [VMEM] * 2,
        out_specs=VMEM,
        scratch_shapes=[pltpu.VMEM((2, n, n), jnp.float32)],
        name="factor_second",
        compiler_params=GRANT,
        cost_estimate=cost(8 * 10**9),
    )(at, state, energies)


def cross_kernel(rows_ref, prev_ref, lead_ref, out_ref):
    out_ref[0] = outer_tile(rows_ref[...], lead_ref[...])
    out_ref[1] = outer_tile(prev_ref[...], lead_ref[...])


def cross(rows, prev_rows, lead_rows):
    n = rows.shape[0]
    return pl.pallas_call(
        cross_kernel,
        out_shape=f32(2, n, n),
        in_specs=[VMEM] * 3,
        out_specs=VMEM,
        name="cross",
        compiler_params=GRANT,
        cost_estimate=cost(10**9),
    )(rows, prev_rows, lead_rows)


def finish_kernel(
    at_ref, own_ref, other_ref, self_ref, cycle_ref, energy_ref, mine_ref, twin_ref,
    panel_ref, energies_ref, diagonal_ref, neighbour_ref, sums_ref, inverse_ref, prev_ref,
):
    n = inverse_ref.shape[0]
    share, half = n // 4, n // 2
    par, core = at_ref[0], at_ref[2]
    inverse_ref[:half, half:] = jnp.zeros((half, half), jnp.float32)
    for i, source in ((0, mine_ref), (1, twin_ref)):
        start = pl.multiple_of(jnp.bitwise_xor(core, i) * share, share)
        inverse_ref[pl.ds(start, share), :half] = source[:share, :]
        inverse_ref[pl.ds(start + half, share), :half] = source[share:half, :]
        inverse_ref[pl.ds(start + half, share), half:] = source[half : half + share, :]
    for i, source in ((0, own_ref), (1, other_ref)):
        start = pl.multiple_of(jnp.bitwise_xor(core, i) * half, half)
        sums_ref[0, pl.ds(start, half), :] = source[0]
        sums_ref[1, pl.ds(start, half), :] = source[1]
    inverse = inverse_ref[...]
    panel = outer_tile(sums_ref[0], inverse)
    panel_ref[...] = panel
    prev_ref[...] = outer_tile(sums_ref[1], inverse)
    start = pl.multiple_of(par * share, share)
    own = panel_ref[pl.ds(start, share), :]
    shifted = (
        lax.broadcasted_iota(jnp.int32, (share, n), 0) + start
        == lax.broadcasted_iota(jnp.int32, (share, n), 1)
    ).astype(jnp.float32)
    diagonal_ref[...] = (
        self_ref[pl.ds(start, share), :] + ridge_shift * shifted - outer_tile(own, panel)
    )
    neighbour_ref[...] = cycle_ref[...] - outer_tile(own, prev_ref[...])
    last = half + share
    lead = jnp.concatenate([mine_ref[last : last + 1, :], mine_ref[last + 1 : last + 2, :]], axis=1)
    remainder = energy_ref[...] - outer_tile(jnp.broadcast_to(lead, (8, n)), panel)[:1]
    energies_ref[...] = jnp.where(at_ref[1] == 0, lead, remainder)


def finish(at, own, other, self_sum, cycle_rows, energies, parts):
    n = self_sum.shape[-1]
    share = n // 4
    return pl.pallas_call(
        finish_kernel,
        out_shape=(f32(n, n), f32(1, n), f32(share, n), f32(share, n)),
        in_specs=[SMEM] + [VMEM] * 7,
        out_specs=(VMEM,) * 4,
        scratch_shapes=[
            pltpu.VMEM((2, n, n), jnp.float32),
            pltpu.VMEM((n, n), jnp.float32),
            pltpu.VMEM((n, n), jnp.float32),
        ],
        name="finish",
        compiler_params=GRANT,
        cost_estimate=cost(10**9),
    )(at, own, other, self_sum, cycle_rows, energies, *parts)


def swapped(value, axis):
    return lax.ppermute(value, axis, [(0, 1), (1, 0)])


def sum_scattered(partials):
    k, n = partials.shape[0], partials.shape[-1]
    quarters = partials.reshape(k, 2, 2, n // 4, n)
    core, xl = lax.axis_index("core"), lax.axis_index("xl")
    pick = lambda a, i, d: lax.dynamic_index_in_dim(a, i, d, keepdims=False)
    halves = pick(quarters, core, 2) + swapped(pick(quarters, 1 - core, 2), "core")
    return pick(halves, xl, 1) + swapped(pick(halves, 1 - xl, 1), "xl")


def sum_halves(partials):
    k, n = partials.shape[0], partials.shape[-1]
    core = lax.axis_index("core")
    chip = partials + swapped(partials, "core")
    halves = chip.reshape(k, 2, n // 2, n)
    own = lax.dynamic_index_in_dim(halves, core, 1, keepdims=False)
    own = own + swapped(own, "xl")
    return own, swapped(own, "core")


SCATTER_ORDER = (6, 2, 5, 7, 1, 3, 4)
STACK_ORDER = (4, 3, 5, 2, 6, 1, 7)


def total(values):
    return functools.reduce(jnp.add, values)


def scatter_lead(rows):
    parts = lax.axis_size(PLANE)
    part = rows.shape[0] // parts
    got = [
        lax.ppermute(rows[k * part : (k + 1) * part], BLK, [(0, k)])
        for k in SCATTER_ORDER
    ]
    return jnp.where(lax.axis_index(PLANE) == 0, rows[:part], total(got))


def along_z(piece):
    got = [lax.ppermute(piece, "z", [(0, k)]) for k in STACK_ORDER]
    return jnp.where(lax.axis_index("z") == 0, piece, total(got))


def over_plane(piece):
    parts = lax.axis_size(PLANE)
    copies = jnp.broadcast_to(piece, (parts, *piece.shape))
    return lax.all_to_all(copies, PLANE, split_axis=0, concat_axis=0, tiled=True)


def small_tree(value):
    z, xh, y = (lax.axis_index(a) for a in BLK)
    rounds = (
        ([[(0, 8 * k)] for k in (4, 2, 6)], z == 0),
        ([[(8 * k, 8 * k + d) for k in range(0, 8, 2)] for d in (4, 12, 8)], (z % 2 == 0) & (xh == 0)),
        ([[(4 * k, 4 * k + d) for k in range(16)] for d in (2, 1, 3)], y == 0),
    )
    for routes, holds in rounds:
        got = [lax.ppermute(value, BLK, route) for route in routes]
        value = jnp.where(holds, value, total(got))
    return value


def on_device(log_derivs, energies):
    n = log_derivs.shape[0]
    energy_row = energies.reshape(1, n)
    at = jnp.stack(
        [lax.axis_index(PAR), lax.axis_index(BLK), lax.axis_index("core")]
    ).astype(jnp.int32)
    wrapped = lax.ppermute(log_derivs, BLK, [(b, (b + 1) % 64) for b in range(3, 64, 4)])
    piece = scatter_lead(log_derivs)
    near = lax.ppermute(log_derivs, BLK, [(b, b + 1) for b in range(64) if b % 4 != 3])
    prev_rows = jnp.where(lax.axis_index("y") == 0, wrapped, near)
    self_part = outer_tile(log_derivs, log_derivs)[None]
    own, other = sum_halves(self_part)
    upper = lax.axis_index("core") == 0
    self_sum = jnp.concatenate(
        [jnp.where(upper, own[0], other[0]), jnp.where(upper, other[0], own[0])]
    )
    piece = along_z(piece)
    state = factor_first(self_sum)
    lead_rows = over_plane(piece).reshape(log_derivs.shape)
    packed = factor_second(at, state, energy_row)
    packed = small_tree(packed)
    twin = swapped(packed, "core")
    cycle_rows = sum_scattered(outer_tile(log_derivs, prev_rows)[None])[0]
    partials = cross(log_derivs, prev_rows, lead_rows)
    own, other = sum_halves(partials)
    panel, energies_next, diagonal, neighbour = finish(
        at, own, other, self_sum, cycle_rows, energy_row, (packed, twin)
    )
    return panel, energies_next.reshape(n), diagonal, neighbour


def solution(mesh):
    torus = Mesh(mesh.devices.reshape(8, 2, 4, 2, 2), ALL)
    in_specs = (P(BLK, PAR), P(BLK))
    out_specs = (P(BLK, None), P(BLK), P(ALL, None), P(ALL, None))
    return jax.shard_map(
        on_device, mesh=torus, in_specs=in_specs, out_specs=out_specs, check_vma=False
    )
```

```python
import functools

import jax
import jax.numpy as jnp
from jax import lax
from jax.experimental import pallas as pl
from jax.experimental.pallas import tpu as pltpu
from jax.sharding import Mesh
from jax.sharding import PartitionSpec as P


BLK = ("z", "xh", "y")
PLANE = ("xh", "y")
PAR = ("xl", "core")
ALL = BLK + PAR
HIGHEST = lax.Precision.HIGHEST


ridge_shift = 0.05
CHUNK = 64
HELPER = 8


def dot(a, b, ca, cb):
    return lax.dot_general(
        a, b, (((ca,), (cb,)), ((), ())), precision=HIGHEST, preferred_element_type=jnp.float32
    )


def outer_tile(left_rows, right_rows):
    return dot(left_rows, right_rows, 1, 1)


def unit(rows, columns):
    return lax.broadcasted_iota(jnp.int32, (rows, columns), 0) == lax.broadcasted_iota(
        jnp.int32, (rows, columns), 1
    )


def triangle_inverse(tile):
    n = tile.shape[0]
    held = jnp.concatenate([tile, unit(n, n).astype(jnp.float32)], axis=1)
    rows = lax.broadcasted_iota(jnp.int32, held.shape, 0)
    for j in range(0, n, 2):
        low = (j // 8) * 8
        part, at = held[low:, :], rows[low:]
        first = jnp.broadcast_to(part[:, j : j + 1], part.shape)
        second = jnp.broadcast_to(part[:, j + 1 : j + 2], part.shape)
        row_a, row_b = held[j : j + 1, :], held[j + 1 : j + 2, :]
        k = j - low
        a, b, c = first[k : k + 1], first[k + 1 : k + 2], second[k + 1 : k + 2]
        over_a = 1.0 / a
        over_det = 1.0 / (a * c - b * b)
        t = b * over_a
        row_b = row_b - t * row_a
        update = first * over_a * row_a + (second - first * t) * (a * over_det) * row_b
        update = jnp.where(at > j + 1, update, 0.0)
        update = jnp.where(at == j + 1, jnp.broadcast_to(t * row_a, part.shape), update)
        part = part - update
        held = jnp.concatenate([held[:low], part], axis=0) if low else part
    pivots = jnp.sum(jnp.where(unit(n, 2 * n), held, 0.0), axis=1, keepdims=True)
    return held[:, n:] * (1.0 / jnp.sqrt(pivots))


def eliminate(tile_ref, inverse_ref, first, last):
    n = tile_ref.shape[0]
    for r0 in range(first * CHUNK, last * CHUNK, CHUNK):
        r1 = r0 + CHUNK
        small = triangle_inverse(tile_ref[r0:r1, r0:r1])
        if r0:
            inverse_ref[r0:r1, :r0] = dot(small, inverse_ref[r0:r1, :r0], 1, 0)
        inverse_ref[r0:r1, r0:r1] = small
        if r1 < n:
            across = dot(small, tile_ref[r0:r1, r1:], 1, 0)
            tile_ref[r1:, r1:] = tile_ref[r1:, r1:] - dot(across, across, 0, 0)
            inverse_ref[r1:, :r1] = inverse_ref[r1:, :r1] - dot(
                across, inverse_ref[r0:r1, :r1], 0, 0
            )


def tile_kernel(rows_ref, energy_ref, out_ref):
    n = rows_ref.shape[0]
    out_ref[:n, :] = outer_tile(rows_ref[...], rows_ref[...])
    out_ref[n:, :] = jnp.broadcast_to(energy_ref[...], (8, n))


def factor_kernel(at_ref, chip_ref, twin_ref, packed_ref, tile_ref, inverse_ref):
    n = tile_ref.shape[0]
    share, half = n // 4, n // 2
    core = at_ref[2]

    @pl.when(at_ref[1] != HELPER)
    def _():
        packed_ref[...] = jnp.zeros(packed_ref.shape, jnp.float32)

    @pl.when(at_ref[1] == HELPER)
    def _():
        tile_ref[...] = chip_ref[:n, :] + twin_ref[:n, :] + ridge_shift * unit(n, n).astype(jnp.float32)
        inverse_ref[...] = jnp.zeros((n, n), jnp.float32)
        eliminate(tile_ref, inverse_ref, 0, n // CHUNK)
        start = pl.multiple_of(core * share, share)
        packed_ref[:share, :] = inverse_ref[pl.ds(start, share), :half]
        packed_ref[share:half, :] = inverse_ref[pl.ds(start + half, share), :half]
        packed_ref[half : half + share, :] = inverse_ref[pl.ds(start + half, share), half:]
        energy = 0.25 * (chip_ref[n:, :] + twin_ref[n:, :])
        lead = outer_tile(energy, inverse_ref[...])
        first = lax.broadcasted_iota(jnp.int32, (8, half), 0) == 0
        packed_ref[half + share :, :] = jnp.where(first, lead[:, :half], lead[:, half:])


VMEM = pl.BlockSpec(memory_space=pltpu.VMEM)
SMEM = pl.BlockSpec(memory_space=pltpu.SMEM)
ANY = pl.BlockSpec(memory_space=pl.ANY)
GRANT = pltpu.CompilerParams(vmem_limit_bytes=16 * 2**20)


def f32(*shape):
    return jax.ShapeDtypeStruct(shape, jnp.float32)


def cost(flops):
    return pl.CostEstimate(flops=flops, bytes_accessed=2**20, transcendentals=0)


def self_tile(rows, energies):
    n = rows.shape[0]
    return pl.pallas_call(
        tile_kernel,
        out_shape=f32(n + 8, n),
        in_specs=[VMEM] * 2,
        out_specs=VMEM,
        name="tile",
        compiler_params=GRANT,
        cost_estimate=cost(10**8),
    )(rows, energies)


def factor(at, chip, twin):
    n = chip.shape[-1]
    return pl.pallas_call(
        factor_kernel,
        out_shape=f32(3 * n // 4 + 8, n // 2),
        in_specs=[SMEM] + [VMEM] * 2,
        out_specs=VMEM,
        scratch_shapes=[pltpu.VMEM((n, n), jnp.float32)] * 2,
        name="factor",
        compiler_params=GRANT,
        cost_estimate=cost(8 * 10**9),
    )(at, chip, twin)


def cross_kernel(rows_ref, prev_ref, lead_ref, out_ref):
    out_ref[0] = outer_tile(rows_ref[...], lead_ref[...])
    out_ref[1] = outer_tile(prev_ref[...], lead_ref[...])


def cross(rows, prev_rows, lead_rows):
    n = rows.shape[0]
    return pl.pallas_call(
        cross_kernel,
        out_shape=f32(2, n, n),
        in_specs=[VMEM] * 3,
        out_specs=VMEM,
        name="cross",
        compiler_params=GRANT,
        cost_estimate=cost(10**9),
    )(rows, prev_rows, lead_rows)


def early_kernel(at_ref, rows_ref, prev_ref, keep_ref, send_ref, tile_ref):
    share = tile_ref.shape[0] // 4
    core = at_ref[2]
    for number, right in ((0, rows_ref), (1, prev_ref)):
        tile_ref[...] = outer_tile(rows_ref[...], right[...])
        for xl in range(2):
            mine = pl.multiple_of((2 * xl + core) * share, share)
            other = pl.multiple_of((2 * xl + 1 - core) * share, share)
            keep_ref[number, xl] = tile_ref[pl.ds(mine, share), :]
            send_ref[number, xl] = tile_ref[pl.ds(other, share), :]


def early_tiles(at, rows, prev_rows):
    n = rows.shape[0]
    return pl.pallas_call(
        early_kernel,
        out_shape=(f32(2, 2, n // 4, n),) * 2,
        in_specs=[SMEM, VMEM, VMEM],
        out_specs=(VMEM,) * 2,
        scratch_shapes=[pltpu.VMEM((n, n), jnp.float32)],
        name="early",
        compiler_params=GRANT,
        cost_estimate=cost(10**9),
    )(at, rows, prev_rows)


def finish_kernel(
    at_ref, own_ref, other_ref, early_ref, energy_ref, mine_ref, twin_ref,
    panel_ref, energies_ref, diagonal_ref, neighbour_ref, sums_ref, inverse_ref, prev_ref,
):
    n = inverse_ref.shape[0]
    share, half = n // 4, n // 2
    par, core = at_ref[0], at_ref[2]
    inverse_ref[:half, half:] = jnp.zeros((half, half), jnp.float32)
    for i, source in ((0, mine_ref), (1, twin_ref)):
        start = pl.multiple_of(jnp.bitwise_xor(core, i) * share, share)
        inverse_ref[pl.ds(start, share), :half] = source[:share, :]
        inverse_ref[pl.ds(start + half, share), :half] = source[share:half, :]
        inverse_ref[pl.ds(start + half, share), half:] = source[half : half + share, :]
    for i, source in ((0, own_ref), (1, other_ref)):
        start = pl.multiple_of(jnp.bitwise_xor(core, i) * half, half)
        sums_ref[0, pl.ds(start, half), :] = source[0]
        sums_ref[1, pl.ds(start, half), :] = source[1]
    inverse = inverse_ref[...]
    panel = outer_tile(sums_ref[0], inverse)
    panel_ref[...] = panel
    prev_ref[...] = outer_tile(sums_ref[1], inverse)
    start = pl.multiple_of(par * share, share)
    own = panel_ref[pl.ds(start, share), :]
    shifted = (
        lax.broadcasted_iota(jnp.int32, (share, n), 0) + start
        == lax.broadcasted_iota(jnp.int32, (share, n), 1)
    ).astype(jnp.float32)
    diagonal_ref[...] = (
        early_ref[0] + ridge_shift * shifted - outer_tile(own, panel)
    )
    neighbour_ref[...] = early_ref[1] - outer_tile(own, prev_ref[...])
    last = half + share
    lead = jnp.concatenate([mine_ref[last : last + 1, :], mine_ref[last + 1 : last + 2, :]], axis=1)
    remainder = energy_ref[...] - outer_tile(jnp.broadcast_to(lead, (8, n)), panel)[:1]
    energies_ref[...] = jnp.where(at_ref[1] == 0, lead, remainder)


def finish(at, own, other, early, energies, parts):
    n = early.shape[-1]
    share = n // 4
    return pl.pallas_call(
        finish_kernel,
        out_shape=(f32(n, n), f32(1, n), f32(share, n), f32(share, n)),
        in_specs=[SMEM] + [VMEM] * 6,
        out_specs=(VMEM,) * 4,
        scratch_shapes=[
            pltpu.VMEM((2, n, n), jnp.float32),
            pltpu.VMEM((n, n), jnp.float32),
            pltpu.VMEM((n, n), jnp.float32),
        ],
        name="finish",
        compiler_params=GRANT,
        cost_estimate=cost(10**9),
    )(at, own, other, early, energies, *parts)


def swapped(value, axis):
    return lax.ppermute(value, axis, [(0, 1), (1, 0)])


def sum_scattered(keep, send):
    xl = lax.axis_index("xl")
    pick = lambda a, i: lax.dynamic_index_in_dim(a, i, 1, keepdims=False)
    halves = keep + swapped(send, "core")
    return pick(halves, xl) + swapped(pick(halves, 1 - xl), "xl")


def lent(value, flip):
    return lax.ppermute(value, ALL, [(p, 4 * HELPER + (p ^ flip)) for p in range(4)])


def helper_swapped(value):
    return lax.ppermute(value, ALL, [(4 * HELPER + p, 4 * HELPER + (p ^ 1)) for p in range(4)])


def sum_halves(partials):
    k, n = partials.shape[0], partials.shape[-1]
    core = lax.axis_index("core")
    chip = partials + swapped(partials, "core")
    halves = chip.reshape(k, 2, n // 2, n)
    own = lax.dynamic_index_in_dim(halves, core, 1, keepdims=False)
    own = own + swapped(own, "xl")
    return own, swapped(own, "core")


SCATTER_ORDER = (6, 2, 5, 7, 1, 3, 4)
STACK_ORDER = (4, 3, 5, 2, 6, 1, 7)


def total(values):
    return functools.reduce(jnp.add, values)


def scatter_lead(rows):
    parts = lax.axis_size(PLANE)
    part = rows.shape[0] // parts
    got = [
        lax.ppermute(rows[k * part : (k + 1) * part], BLK, [(0, k)])
        for k in SCATTER_ORDER
    ]
    return jnp.where(lax.axis_index(PLANE) == 0, rows[:part], total(got))


def along_z(piece):
    got = [lax.ppermute(piece, "z", [(0, k)]) for k in STACK_ORDER]
    return jnp.where(lax.axis_index("z") == 0, piece, total(got))


def over_plane(piece):
    parts = lax.axis_size(PLANE)
    copies = jnp.broadcast_to(piece, (parts, *piece.shape))
    return lax.all_to_all(copies, PLANE, split_axis=0, concat_axis=0, tiled=True)


def small_tree(value):
    z, xh, y = (lax.axis_index(a) for a in BLK)
    ahead = (z + 7) % 8
    at = lambda i: (i + HELPER) % 64
    rounds = (
        ([[(0, 8 * k)] for k in (4, 2, 6)], ahead == 0),
        (
            [[(8 * k, 8 * k + d) for k in range(0, 8, 2)] for d in (4, 12, 8)],
            (ahead % 2 == 0) & (xh == 0),
        ),
        ([[(4 * k, 4 * k + d) for k in range(16)] for d in (2, 1, 3)], y == 0),
    )
    for routes, holds in rounds:
        got = [
            lax.ppermute(value, BLK, [(at(i), at(k)) for i, k in route]) for route in routes
        ]
        value = jnp.where(holds, value, total(got))
    return value


def on_device(log_derivs, energies):
    n = log_derivs.shape[0]
    energy_row = energies.reshape(1, n)
    at = jnp.stack(
        [lax.axis_index(a) for a in (PAR, BLK, "core", "y")]
    ).astype(jnp.int32)
    wrapped = lax.ppermute(log_derivs, BLK, [(b, (b + 1) % 64) for b in range(3, 64, 4)])
    self_part = self_tile(log_derivs, energy_row)
    chip = lent(self_part, 0) + lent(self_part, 2)
    piece = scatter_lead(log_derivs)
    near = lax.ppermute(log_derivs, BLK, [(b, b + 1) for b in range(64) if b % 4 != 3])
    twin = helper_swapped(chip)
    piece = along_z(piece)
    packed = factor(at, chip, twin)
    lead_rows = over_plane(piece).reshape(log_derivs.shape)
    packed = small_tree(packed)
    twin = swapped(packed, "core")
    prev_rows = jnp.where(lax.axis_index("y") == 0, wrapped, near)
    keep, send = early_tiles(at, log_derivs, prev_rows)
    early = sum_scattered(keep, send)
    partials = cross(log_derivs, prev_rows, lead_rows)
    own, other = sum_halves(partials)
    panel, energies_next, diagonal, neighbour = finish(
        at, own, other, early, energy_row, (packed, twin)
    )
    return panel, energies_next.reshape(n), diagonal, neighbour


def solution(mesh):
    torus = Mesh(mesh.devices.reshape(8, 2, 4, 2, 2), ALL)
    in_specs = (P(BLK, PAR), P(BLK))
    out_specs = (P(BLK, None), P(BLK), P(ALL, None), P(ALL, None))
    return jax.shard_map(
        on_device, mesh=torus, in_specs=in_specs, out_specs=out_specs, check_vma=False
    )
```

```python
import functools

import jax
import jax.numpy as jnp
from jax import lax
from jax.experimental import pallas as pl
from jax.experimental.pallas import tpu as pltpu
from jax.sharding import Mesh
from jax.sharding import PartitionSpec as P


BLK = ("z", "xh", "y")
PLANE = ("xh", "y")
PAR = ("xl", "core")
ALL = BLK + PAR
HIGHEST = lax.Precision.HIGHEST


ridge_shift = 0.05
CHUNK = 64
HELPER = 8


def dot(a, b, ca, cb):
    return lax.dot_general(
        a, b, (((ca,), (cb,)), ((), ())), precision=HIGHEST, preferred_element_type=jnp.float32
    )


def outer_tile(left_rows, right_rows):
    return dot(left_rows, right_rows, 1, 1)


def unit(rows, columns):
    return lax.broadcasted_iota(jnp.int32, (rows, columns), 0) == lax.broadcasted_iota(
        jnp.int32, (rows, columns), 1
    )


def triangle_inverse(tile):
    n = tile.shape[0]
    held = jnp.concatenate([tile, unit(n, n).astype(jnp.float32)], axis=1)
    rows = lax.broadcasted_iota(jnp.int32, (8, 2 * n), 0)
    for j in range(0, n, 4):
        low = (j // 8) * 8
        k = j - low
        part = held[low:, :]
        column = [jnp.broadcast_to(part[:, j + m : j + m + 1], part.shape) for m in range(4)]
        row = [held[j + m : j + m + 1, :] for m in range(4)]
        entry = lambda i, m: column[m][k + i : k + i + 1]
        over_0 = 1.0 / entry(0, 0)
        t = entry(1, 0) * over_0
        over_1 = entry(0, 0) * (
            1.0 / (entry(0, 0) * entry(1, 1) - entry(1, 0) * entry(1, 0))
        )
        row_1 = row[1] - t * row[0]
        rest_2, rest_3 = entry(2, 1) - t * entry(2, 0), entry(3, 1) - t * entry(3, 0)
        g20, g30 = entry(2, 0) * over_0, entry(3, 0) * over_0
        g21, g31 = rest_2 * over_1, rest_3 * over_1
        row_2 = row[2] - g20 * row[0] - g21 * row_1
        row_3 = row[3] - g30 * row[0] - g31 * row_1
        b22 = entry(2, 2) - g20 * entry(2, 0) - g21 * rest_2
        b32 = entry(3, 2) - g30 * entry(2, 0) - g31 * rest_2
        b33 = entry(3, 3) - g30 * entry(3, 0) - g31 * rest_3
        over_2 = 1.0 / b22
        s = b32 * over_2
        over_3 = b22 * (1.0 / (b22 * b33 - b32 * b32))
        row_3 = row_3 - s * row_2
        f0 = column[0] * over_0
        f1 = (column[1] - column[0] * t) * over_1
        left_2 = column[2] - f0 * entry(2, 0) - f1 * rest_2
        left_3 = column[3] - f0 * entry(3, 0) - f1 * rest_3
        f2 = left_2 * over_2
        f3 = (left_3 - left_2 * s) * over_3
        new = part - (f0 * row[0] + f1 * row_1 + f2 * row_2 + f3 * row_3)
        head = jnp.where(rows > k + 3, new[:8], part[:8])
        for m, value in ((1, row_1), (2, row_2), (3, row_3)):
            head = jnp.where(rows == k + m, jnp.broadcast_to(value, head.shape), head)
        pieces = ([held[:low]] if low else []) + [head] + ([new[8:]] if low + 8 < n else [])
        held = jnp.concatenate(pieces, axis=0) if len(pieces) > 1 else head
    pivots = jnp.sum(jnp.where(unit(n, 2 * n), held, 0.0), axis=1, keepdims=True)
    return held[:, n:] * (1.0 / jnp.sqrt(pivots))


def eliminate(tile_ref, inverse_ref, first, last):
    n = tile_ref.shape[0]
    for r0 in range(first * CHUNK, last * CHUNK, CHUNK):
        r1 = r0 + CHUNK
        small = triangle_inverse(tile_ref[r0:r1, r0:r1])
        if r0:
            inverse_ref[r0:r1, :r0] = dot(small, inverse_ref[r0:r1, :r0], 1, 0)
        inverse_ref[r0:r1, r0:r1] = small
        if r1 < n:
            across = dot(small, tile_ref[r0:r1, r1:], 1, 0)
            tile_ref[r1:, r1:] = tile_ref[r1:, r1:] - dot(across, across, 0, 0)
            inverse_ref[r1:, :r1] = inverse_ref[r1:, :r1] - dot(
                across, inverse_ref[r0:r1, :r1], 0, 0
            )


def tile_kernel(rows_ref, energy_ref, out_ref):
    n = rows_ref.shape[0]
    out_ref[:n, :] = outer_tile(rows_ref[...], rows_ref[...])
    out_ref[n:, :] = jnp.broadcast_to(energy_ref[...], (8, n))


def factor_kernel(at_ref, chip_ref, twin_ref, packed_ref, tile_ref, inverse_ref):
    n = tile_ref.shape[0]
    share, half = n // 4, n // 2
    core = at_ref[2]

    @pl.when(at_ref[1] != HELPER)
    def _():
        packed_ref[...] = jnp.zeros(packed_ref.shape, jnp.float32)

    @pl.when(at_ref[1] == HELPER)
    def _():
        tile_ref[...] = chip_ref[:n, :] + twin_ref[:n, :] + ridge_shift * unit(n, n).astype(jnp.float32)
        inverse_ref[...] = jnp.zeros((n, n), jnp.float32)
        eliminate(tile_ref, inverse_ref, 0, n // CHUNK)
        start = pl.multiple_of(core * share, share)
        packed_ref[:share, :] = inverse_ref[pl.ds(start, share), :half]
        packed_ref[share:half, :] = inverse_ref[pl.ds(start + half, share), :half]
        packed_ref[half : half + share, :] = inverse_ref[pl.ds(start + half, share), half:]
        energy = 0.25 * (chip_ref[n:, :] + twin_ref[n:, :])
        lead = outer_tile(energy, inverse_ref[...])
        first = lax.broadcasted_iota(jnp.int32, (8, half), 0) == 0
        packed_ref[half + share :, :] = jnp.where(first, lead[:, :half], lead[:, half:])


VMEM = pl.BlockSpec(memory_space=pltpu.VMEM)
SMEM = pl.BlockSpec(memory_space=pltpu.SMEM)
ANY = pl.BlockSpec(memory_space=pl.ANY)
GRANT = pltpu.CompilerParams(vmem_limit_bytes=16 * 2**20)


def f32(*shape):
    return jax.ShapeDtypeStruct(shape, jnp.float32)


def cost(flops):
    return pl.CostEstimate(flops=flops, bytes_accessed=2**20, transcendentals=0)


def self_tile(rows, energies):
    n = rows.shape[0]
    return pl.pallas_call(
        tile_kernel,
        out_shape=f32(n + 8, n),
        in_specs=[VMEM] * 2,
        out_specs=VMEM,
        name="tile",
        compiler_params=GRANT,
        cost_estimate=cost(10**8),
    )(rows, energies)


def factor(at, chip, twin):
    n = chip.shape[-1]
    return pl.pallas_call(
        factor_kernel,
        out_shape=f32(3 * n // 4 + 8, n // 2),
        in_specs=[SMEM] + [VMEM] * 2,
        out_specs=VMEM,
        scratch_shapes=[pltpu.VMEM((n, n), jnp.float32)] * 2,
        name="factor",
        compiler_params=GRANT,
        cost_estimate=cost(8 * 10**9),
    )(at, chip, twin)


def cross_kernel(rows_ref, prev_ref, lead_ref, out_ref):
    out_ref[0] = outer_tile(rows_ref[...], lead_ref[...])
    out_ref[1] = outer_tile(prev_ref[...], lead_ref[...])


def cross(rows, prev_rows, lead_rows):
    n = rows.shape[0]
    return pl.pallas_call(
        cross_kernel,
        out_shape=f32(2, n, n),
        in_specs=[VMEM] * 3,
        out_specs=VMEM,
        name="cross",
        compiler_params=GRANT,
        cost_estimate=cost(10**9),
    )(rows, prev_rows, lead_rows)


def early_kernel(at_ref, rows_ref, prev_ref, keep_ref, send_ref, tile_ref):
    share = tile_ref.shape[0] // 4
    core = at_ref[2]
    for number, right in ((0, rows_ref), (1, prev_ref)):
        tile_ref[...] = outer_tile(rows_ref[...], right[...])
        for xl in range(2):
            mine = pl.multiple_of((2 * xl + core) * share, share)
            other = pl.multiple_of((2 * xl + 1 - core) * share, share)
            keep_ref[number, xl] = tile_ref[pl.ds(mine, share), :]
            send_ref[number, xl] = tile_ref[pl.ds(other, share), :]


def early_tiles(at, rows, prev_rows):
    n = rows.shape[0]
    return pl.pallas_call(
        early_kernel,
        out_shape=(f32(2, 2, n // 4, n),) * 2,
        in_specs=[SMEM, VMEM, VMEM],
        out_specs=(VMEM,) * 2,
        scratch_shapes=[pltpu.VMEM((n, n), jnp.float32)],
        name="early",
        compiler_params=GRANT,
        cost_estimate=cost(10**9),
    )(at, rows, prev_rows)


def finish_kernel(
    at_ref, own_ref, other_ref, early_ref, energy_ref, mine_ref, twin_ref,
    panel_ref, energies_ref, diagonal_ref, neighbour_ref, sums_ref, inverse_ref, prev_ref,
):
    n = inverse_ref.shape[0]
    share, half = n // 4, n // 2
    par, core = at_ref[0], at_ref[2]
    inverse_ref[:half, half:] = jnp.zeros((half, half), jnp.float32)
    for i, source in ((0, mine_ref), (1, twin_ref)):
        start = pl.multiple_of(jnp.bitwise_xor(core, i) * share, share)
        inverse_ref[pl.ds(start, share), :half] = source[:share, :]
        inverse_ref[pl.ds(start + half, share), :half] = source[share:half, :]
        inverse_ref[pl.ds(start + half, share), half:] = source[half : half + share, :]
    for i, source in ((0, own_ref), (1, other_ref)):
        start = pl.multiple_of(jnp.bitwise_xor(core, i) * half, half)
        sums_ref[0, pl.ds(start, half), :] = source[0]
        sums_ref[1, pl.ds(start, half), :] = source[1]
    inverse = inverse_ref[...]
    panel = outer_tile(sums_ref[0], inverse)
    panel_ref[...] = panel
    prev_ref[...] = outer_tile(sums_ref[1], inverse)
    start = pl.multiple_of(par * share, share)
    own = panel_ref[pl.ds(start, share), :]
    shifted = (
        lax.broadcasted_iota(jnp.int32, (share, n), 0) + start
        == lax.broadcasted_iota(jnp.int32, (share, n), 1)
    ).astype(jnp.float32)
    diagonal_ref[...] = (
        early_ref[0] + ridge_shift * shifted - outer_tile(own, panel)
    )
    neighbour_ref[...] = early_ref[1] - outer_tile(own, prev_ref[...])
    last = half + share
    lead = jnp.concatenate([mine_ref[last : last + 1, :], mine_ref[last + 1 : last + 2, :]], axis=1)
    remainder = energy_ref[...] - outer_tile(jnp.broadcast_to(lead, (8, n)), panel)[:1]
    energies_ref[...] = jnp.where(at_ref[1] == 0, lead, remainder)


def finish(at, own, other, early, energies, parts):
    n = early.shape[-1]
    share = n // 4
    return pl.pallas_call(
        finish_kernel,
        out_shape=(f32(n, n), f32(1, n), f32(share, n), f32(share, n)),
        in_specs=[SMEM] + [VMEM] * 6,
        out_specs=(VMEM,) * 4,
        scratch_shapes=[
            pltpu.VMEM((2, n, n), jnp.float32),
            pltpu.VMEM((n, n), jnp.float32),
            pltpu.VMEM((n, n), jnp.float32),
        ],
        name="finish",
        compiler_params=GRANT,
        cost_estimate=cost(10**9),
    )(at, own, other, early, energies, *parts)


def swapped(value, axis):
    return lax.ppermute(value, axis, [(0, 1), (1, 0)])


def sum_scattered(keep, send):
    xl = lax.axis_index("xl")
    pick = lambda a, i: lax.dynamic_index_in_dim(a, i, 1, keepdims=False)
    halves = keep + swapped(send, "core")
    return pick(halves, xl) + swapped(pick(halves, 1 - xl), "xl")


def lent(value, flip):
    return lax.ppermute(value, ALL, [(p, 4 * HELPER + (p ^ flip)) for p in range(4)])


def helper_swapped(value):
    return lax.ppermute(value, ALL, [(4 * HELPER + p, 4 * HELPER + (p ^ 1)) for p in range(4)])


def sum_halves(partials):
    k, n = partials.shape[0], partials.shape[-1]
    core = lax.axis_index("core")
    chip = partials + swapped(partials, "core")
    halves = chip.reshape(k, 2, n // 2, n)
    own = lax.dynamic_index_in_dim(halves, core, 1, keepdims=False)
    own = own + swapped(own, "xl")
    return own, swapped(own, "core")


SCATTER_ORDER = (6, 2, 5, 7, 1, 3, 4)
STACK_ORDER = (4, 3, 5, 2, 6, 1, 7)


def total(values):
    return functools.reduce(jnp.add, values)


def scatter_lead(rows):
    parts = lax.axis_size(PLANE)
    part = rows.shape[0] // parts
    got = [
        lax.ppermute(rows[k * part : (k + 1) * part], BLK, [(0, k)])
        for k in SCATTER_ORDER
    ]
    return jnp.where(lax.axis_index(PLANE) == 0, rows[:part], total(got))


def along_z(piece):
    got = [lax.ppermute(piece, "z", [(0, k)]) for k in STACK_ORDER]
    return jnp.where(lax.axis_index("z") == 0, piece, total(got))


def over_plane(piece):
    parts = lax.axis_size(PLANE)
    copies = jnp.broadcast_to(piece, (parts, *piece.shape))
    return lax.all_to_all(copies, PLANE, split_axis=0, concat_axis=0, tiled=True)


def small_tree(value):
    z, xh, y = (lax.axis_index(a) for a in BLK)
    ahead = (z + 7) % 8
    at = lambda i: (i + HELPER) % 64
    rounds = (
        ([[(0, 8 * k)] for k in (4, 2, 6)], ahead == 0),
        (
            [[(8 * k, 8 * k + d) for k in range(0, 8, 2)] for d in (4, 12, 8)],
            (ahead % 2 == 0) & (xh == 0),
        ),
        ([[(4 * k, 4 * k + d) for k in range(16)] for d in (2, 1, 3)], y == 0),
    )
    for routes, holds in rounds:
        got = [
            lax.ppermute(value, BLK, [(at(i), at(k)) for i, k in route]) for route in routes
        ]
        value = jnp.where(holds, value, total(got))
    return value


def on_device(log_derivs, energies):
    n = log_derivs.shape[0]
    energy_row = energies.reshape(1, n)
    at = jnp.stack(
        [lax.axis_index(a) for a in (PAR, BLK, "core", "y")]
    ).astype(jnp.int32)
    wrapped = lax.ppermute(log_derivs, BLK, [(b, (b + 1) % 64) for b in range(3, 64, 4)])
    self_part = self_tile(log_derivs, energy_row)
    chip = lent(self_part, 0) + lent(self_part, 2)
    piece = scatter_lead(log_derivs)
    near = lax.ppermute(log_derivs, BLK, [(b, b + 1) for b in range(64) if b % 4 != 3])
    twin = helper_swapped(chip)
    piece = along_z(piece)
    packed = factor(at, chip, twin)
    lead_rows = over_plane(piece).reshape(log_derivs.shape)
    packed = small_tree(packed)
    twin = swapped(packed, "core")
    prev_rows = jnp.where(lax.axis_index("y") == 0, wrapped, near)
    keep, send = early_tiles(at, log_derivs, prev_rows)
    early = sum_scattered(keep, send)
    partials = cross(log_derivs, prev_rows, lead_rows)
    own, other = sum_halves(partials)
    panel, energies_next, diagonal, neighbour = finish(
        at, own, other, early, energy_row, (packed, twin)
    )
    return panel, energies_next.reshape(n), diagonal, neighbour


def solution(mesh):
    torus = Mesh(mesh.devices.reshape(8, 2, 4, 2, 2), ALL)
    in_specs = (P(BLK, PAR), P(BLK))
    out_specs = (P(BLK, None), P(BLK), P(ALL, None), P(ALL, None))
    return jax.shard_map(
        on_device, mesh=torus, in_specs=in_specs, out_specs=out_specs, check_vma=False
    )
```
